256 devices in a mesh: seq: 64 (over x, z, core), head: 4 (over y).
Axes of the slice: x: 4, y: 4, z: 8, core: 2. Of those that a mesh axis runs over, the one named last changes fastest.
Arguments:
- query: bfloat16 [16384, 8192], P('seq', 'head'), may hold values from -6 to 6
- key_rows: bfloat16 [16384, 8192], P('seq', 'head'), may hold values from -6 to 6
- value_rows: bfloat16 [16384, 8192], P('seq', 'head'), may hold values from -6 to 6
- head_norm_gain: float32 [8192], P('head'), may hold values from 0.25 to 1.75
- decay_level: int32 [64], P('head'), may hold values from 0 to 11
- routing: int32 [16384, 2], P('seq'), may hold values from 0 to 31, all different within a row; in each aligned block of 256 rows (0 to 255, 256 to 511, ...) at most 24 rows name the same one
Outputs:
- dispatched: bfloat16 [32, 1536, 8192], P('head', 'seq')
The draws below stay inside these ranges and needn't reach their ends.
Inputs may be any that keep to these rules, and one draw needn't show every extreme that they name: `routing`: each token names 2 different experts; among the 256 tokens of one index of seq no expert is named more than 24 times, and in every draw some expert is named exactly 24 times.
All inputs are finite; a program needn't handle non-finite values.
Results may differ from the reference program's by a relative error of at most 0.0049.
Values may be sent and summed in bfloat16 or wider, within the bound.
A program may use at most 192 MiB of HBM per device.

```python
import math
import jax
import jax.numpy as jnp
import numpy as np
from jax import lax

HEADS = 64
HD = 128
EXPERTS = 32
TOP = 2
TOK_DEV = 256
CAP = 24
TOKENS = 16384
SLOTS = 1536


def plant(array, rng, low, high):
    index_at = [jax.random.randint(jax.random.fold_in(rng, axis), (), 0, length) for axis, length in enumerate(array.shape)]
    widest = array.shape.index(max(array.shape))
    beside = index_at[:widest] + [(index_at[widest] + 1) % array.shape[widest]] + index_at[widest + 1:]
    return array.at[tuple(index_at)].set(low).at[tuple(beside)].set(high)


def block_scale(key, extent, shards, smallest, high):
    level = 1.0
    for axis_at, blocks in shards:
        heights = jax.random.uniform(jax.random.fold_in(jax.random.fold_in(key, 6), axis_at), (blocks,), jnp.float32, smallest / len(shards), high / len(shards))
        level = level * jnp.repeat(jnp.exp(heights), extent[axis_at] // blocks).reshape((-1,) + (1,) * (len(extent) - 1 - axis_at))
    return level


def assign_block(rng, own, number, rows, amount, top, most, skew):
    order = jax.random.permutation(rng, amount)
    crowded, usual = portions_of(amount, rows * top, most, skew, True), portions_of(amount, rows * top, most, skew, False)
    places = jnp.arange(amount)

    def named(tallies, rotation):
        used = int((tallies > 0).sum())
        fixed = max(1, used // 4)
        shifted = fixed + (places - fixed + rotation * (used - fixed)) % max(1, amount - fixed)
        return jnp.zeros((amount,), jnp.int32).at[order[jnp.where(places < fixed, places, shifted)]].set(jnp.asarray(tallies, jnp.int32))

    tallies = jnp.where(number % 4 == 0, named(crowded, number // 4), named(usual, number - number // 4 - 1))
    mixed = jax.random.permutation(jax.random.fold_in(own, 3), amount)
    source_of, receiver = mixed[0:amount // 2 * 2:2], mixed[1:amount // 2 * 2:2]
    room = jnp.minimum(tallies[source_of] - 1, most - tallies[receiver]) // 2
    room = jnp.where((source_of == order[0]) | (receiver == order[0]) | (tallies[receiver] == 0), 0, jnp.maximum(room, 0))
    shifted = jax.random.randint(jax.random.fold_in(own, 4), (amount // 2,), 0, 1 << 20) % (room + 1)
    tallies = tallies.at[source_of].add(-shifted).at[receiver].add(shifted)
    items = jnp.searchsorted(jnp.cumsum(tallies), jnp.arange(rows * top), side="right").astype(jnp.int32)
    listing = items.reshape(top, rows).T
    listing = listing[jax.random.permutation(jax.random.fold_in(own, 1), rows)]
    rotation = jax.random.randint(jax.random.fold_in(own, 2), (rows, 1), 0, top)
    return jnp.take_along_axis(listing, (jnp.arange(top)[None, :] + rotation) % top, axis=1)


def portions_of(number_of, total, most, skew, full):
    portions = [(1 << 20) // math.isqrt(grade ** skew) + 1 for grade in range(1, number_of + 1)]
    largest = most if full else min(most, max(-(-total // number_of), total * portions[0] // sum(portions)))
    least = 1 if total - largest >= number_of - 1 else 0
    holding, surplus = [largest] + [least] * (number_of - 1), total - largest - least * (number_of - 1)
    while surplus > 0:
        free = [i for i in range(1, number_of) if holding[i] < largest] or [i for i in range(1, number_of) if holding[i] < most]
        pool, left = sum([portions[i] for i in free]), surplus
        for i in free:
            addition = min(most - holding[i], max(1, left * portions[i] // pool), surplus)
            holding[i] = holding[i] + addition
            surplus = surplus - addition
    return np.array(holding)


def gaussian(own_key, extent, width, most, cuts=(), dtype=jnp.bfloat16):
    values = jax.random.normal(own_key, extent, jnp.float32) * width
    if len(cuts) > 0:
        values = block_scale(own_key, extent, cuts, -0.22, 0.18) * values
    return jnp.clip(values, min=-most, max=most).astype(dtype)


def setup_inputs(seed: int = 0) -> dict:
    key_of = jax.random.split(jax.random.key(seed), 7)
    query = gaussian(key_of[0], (TOKENS, HEADS * HD), 1.0, 6.0, ((0, 64), (1, 4)))
    key_rows = gaussian(key_of[1], (TOKENS, HEADS * HD), 1.0, 6.0, ((0, 64), (1, 4)))
    value_rows = gaussian(key_of[2], (TOKENS, HEADS * HD), 1.0, 6.0, ((0, 64), (1, 4)))
    head_norm_gain = jnp.clip(1.0 + 0.15 * jax.random.normal(key_of[3], (HEADS * HD,), jnp.float32), 0.25, 1.75)
    decay_level = plant(jax.random.randint(key_of[4], (HEADS,), 0, 12), jax.random.fold_in(key_of[4], 1), 0, 11).astype(jnp.int32)
    routing_keys = jax.random.split(jax.random.fold_in(key_of[5], 1), TOKENS // TOK_DEV)
    routing_turns = jax.random.permutation(jax.random.fold_in(key_of[5], 3), TOKENS // TOK_DEV)
    routing = jax.vmap(lambda own, number: assign_block(jax.random.fold_in(key_of[5], 2), own, number, TOK_DEV, EXPERTS, TOP, CAP, 1))(routing_keys, routing_turns).reshape((TOKENS, TOP))
    return {"query": query, "key_rows": key_rows, "value_rows": value_rows, "head_norm_gain": head_norm_gain, "decay_level": decay_level, "routing": routing}


def reference(query, key_rows, value_rows, head_norm_gain, decay_level, routing):
    seq_count = TOKENS // TOK_DEV
    rate = jnp.exp2(decay_level.astype(jnp.float32) - 2.0) / TOKENS
    place = jnp.arange(TOK_DEV).astype(jnp.float32)
    gain_heads = head_norm_gain.reshape(HEADS, HD)
    decay_in = jnp.exp(-rate[None, :] * (place[:, None] + 1.0))
    decay_out = jnp.exp(-rate[None, :] * (TOK_DEV - 1.0 - place[:, None]))
    offset = place[:, None] - place[None, :]
    causal = offset >= 0
    mask_decay = jnp.where(causal[None, :, :], jnp.exp(-rate[:, None, None] * jnp.maximum(offset, 0.0)[None, :, :]), 0.0)
    block_decay = jnp.exp(-rate * TOK_DEV)

    def one_block(state, pieces):
        query_tile, key_block, value_block = pieces
        query_head_rows = query_tile.reshape(TOK_DEV, HEADS, HD).astype(jnp.float32)
        key_head_rows = key_block.reshape(TOK_DEV, HEADS, HD).astype(jnp.float32)
        value_heads = value_block.reshape(TOK_DEV, HEADS, HD).astype(jnp.float32)
        inter = jnp.einsum('lhd,hde->lhe', query_head_rows, state, precision=lax.Precision.HIGHEST) * decay_in[:, :, None]
        attention_scores = jnp.einsum('bjt,rjt->jbr', query_head_rows, key_head_rows)
        weights = (attention_scores * mask_decay).astype(jnp.bfloat16)
        intra = jnp.einsum('hlm,mhe->lhe', weights.astype(jnp.float32), value_heads)
        attended = inter + intra
        scale = lax.rsqrt(lax.optimization_barrier(jnp.mean(attended * attended, axis=-1, keepdims=True)) + 1e-05)
        normed = (attended * scale * gain_heads[None, :, :]).astype(jnp.bfloat16)
        weighted_keys = (key_head_rows * decay_out[:, :, None]).astype(jnp.bfloat16)
        block_state = jnp.einsum('lhd,lhe->hde', weighted_keys.astype(jnp.float32), value_heads)
        new_state = block_decay[:, None, None] * state + block_state
        return (new_state, normed.reshape(TOK_DEV, HEADS * HD))
    start = jnp.zeros((HEADS, HD, HD), jnp.float32)
    blocks = (query.reshape(seq_count, TOK_DEV, HEADS * HD), key_rows.reshape(seq_count, TOK_DEV, HEADS * HD), value_rows.reshape(seq_count, TOK_DEV, HEADS * HD))
    final_state, normed_all = lax.scan(one_block, start, blocks)
    normed_all = normed_all.reshape(TOKENS, HEADS * HD)
    flat_routes = routing.reshape(seq_count, TOK_DEV * TOP)
    onehot = (flat_routes[:, :, None] == jnp.arange(EXPERTS).astype(jnp.int32)[None, None, :]).astype(jnp.int32)
    before = jnp.cumsum(onehot, axis=1) - onehot
    slot = lax.optimization_barrier(jnp.sum(before * onehot, axis=-1))
    block_index = jnp.arange(seq_count).astype(jnp.int32)[:, None]
    target_slot = (block_index * CAP + slot).reshape(-1)
    token_index = (block_index * TOK_DEV + (jnp.arange(TOK_DEV * TOP).astype(jnp.int32) // TOP)[None, :]).reshape(-1)
    experts_flat = flat_routes.reshape(-1)
    dispatched = jnp.zeros((EXPERTS, SLOTS, HEADS * HD), jnp.bfloat16)
    dispatched = dispatched.at[experts_flat, target_slot].set(normed_all[token_index])
    return dispatched
```

```python
import functools

import jax
import jax.numpy as jnp
from jax import lax
from jax.experimental import pallas as pl
from jax.experimental.pallas import tpu as pltpu
from jax.sharding import PartitionSpec as P

EXPERTS = 32
CAP = 24
HD = 128
ROW = 16
GROUPS = 4
MESH = pl.DeviceIdType.MESH
F32 = jnp.float32
BF16 = jnp.bfloat16


def kernel(
    sizes,
    level_ref,
    routing_ref,
    gain_ref,
    q_hbm,
    k_hbm,
    v_hbm,
    out_ref,
    q_ref,
    k_ref,
    v_ref,
    state_ref,
    rows_ref,
    total_ref,
    back_ref,
    incoming_ref,
    intra_ref,
    pick_ref,
    picked_ref,
    block_decay_ref,
    row_decay_ref,
    load_sem,
    row_sem,
    total_sem,
    back_sem,
    out_sem,
):
    length, heads, seq_count, head_count = sizes
    across = seq_count // ROW
    per_group = heads // GROUPS
    width = per_group * HD
    piece = width // ROW
    features = heads * HD
    seats = EXPERTS // head_count * CAP

    seq = lax.axis_index("seq")
    me_head = lax.axis_index("head")
    me_row = lax.rem(seq, ROW)
    me_x = lax.div(seq, ROW)
    row_base = me_x * ROW

    loads = []
    for g in range(GROUPS):
        cols = pl.ds(g * width, width)
        loads.append([
            pltpu.make_async_copy(k_hbm.at[:, cols], k_ref.at[:, cols], load_sem.at[0, g]),
            pltpu.make_async_copy(v_hbm.at[:, cols], v_ref.at[:, cols], load_sem.at[1, g]),
        ])
    for pair in loads:
        for copy in pair:
            copy.start()
    q_load = pltpu.make_async_copy(q_hbm, q_ref, load_sem.at[2, 0])
    q_load.start()

    barrier = pltpu.get_barrier_semaphore()

    def greet(device):
        pl.semaphore_signal(barrier, inc=1, device_id=device, device_id_type=MESH)

    def row_peer(d):
        return lax.rem(me_row + d, ROW)

    def x_peer(d):
        return lax.rem(me_x + d, across)

    def head_peer(d):
        return lax.rem(me_head + d, head_count)

    @pl.loop(1, ROW)
    def _(d):
        greet((row_base + row_peer(d), me_head))

    for d in range(1, across):
        greet((x_peer(d) * ROW + me_row, me_head))
    for d in range(1, head_count):
        greet((seq, head_peer(d)))

    def rate_row(h, n):
        level = jnp.full((1, n), level_ref[h], jnp.int32)
        return jnp.exp2(level.astype(F32) - 2.0) / (length * seq_count)

    for h in range(heads):
        rate = rate_row(h, HD)
        block_decay_ref[h] = jnp.broadcast_to(jnp.exp(-rate * length), (8, HD))
        row_decay_ref[h] = jnp.broadcast_to(jnp.exp(-rate * (length * ROW)), (8, HD))

    place = lax.broadcasted_iota(jnp.int32, (length, HD), 0).astype(F32)

    def head_cols(h):
        return pl.ds(h * HD, HD)

    def state(h):
        g, at = divmod(h, per_group)
        decay_out = jnp.exp(-rate_row(h, HD) * (length - 1.0 - place))
        weighted = (k_ref[:, head_cols(h)].astype(F32) * decay_out).astype(BF16)
        made = lax.dot_general(
            weighted, v_ref[:, head_cols(h)], (((0,), (0,)), ((), ())), preferred_element_type=F32
        )
        state_ref[g, pl.ds(at * HD, HD), :] = made.astype(BF16)

    def at_piece(r):
        return pl.ds(pl.multiple_of(r * piece, piece), piece)

    def row_copy(g, to):
        return pltpu.make_async_remote_copy(
            src_ref=state_ref.at[g, at_piece(to), :],
            dst_ref=rows_ref.at[g, at_piece(me_row), :],
            send_sem=row_sem.at[0, g],
            recv_sem=row_sem.at[1, g],
            device_id=(row_base + to, me_head),
            device_id_type=MESH,
        )

    def send_row(g):
        @pl.loop(1, ROW)
        def _(d):
            row_copy(g, row_peer(d)).start()

        rows_ref[g, at_piece(me_row), :] = state_ref[g, at_piece(me_row), :]

    def wait_bytes(ref, sem):
        pltpu.make_async_copy(ref, ref, sem).wait()

    others = pl.ds(0, (ROW - 1) * piece)

    def decays(ref, g):
        return jnp.broadcast_to(ref[g * per_group + lax.div(me_row * piece, HD)][0:1], (piece, HD))

    def total_copy(g, to):
        return pltpu.make_async_remote_copy(
            src_ref=total_ref.at[g, me_x],
            dst_ref=total_ref.at[g, me_x],
            send_sem=total_sem.at[0, g],
            recv_sem=total_sem.at[1, g],
            device_id=(to * ROW + me_row, me_head),
            device_id_type=MESH,
        )

    def sum_row(g):
        wait_bytes(rows_ref.at[g, others], row_sem.at[1, g])
        decay = decays(block_decay_ref, g)
        carried = jnp.zeros((piece, HD), F32)
        for r in range(ROW):
            carried = decay * carried + rows_ref[g, pl.ds(r * piece, piece), :].astype(F32)
        total_ref[g, me_x] = carried
        for d in range(1, across):
            total_copy(g, x_peer(d)).start()

    def back_copy(g, to):
        return pltpu.make_async_remote_copy(
            src_ref=back_ref.at[g, at_piece(to), :],
            dst_ref=incoming_ref.at[g, at_piece(me_row), :],
            send_sem=back_sem.at[0, g],
            recv_sem=back_sem.at[1, g],
            device_id=(row_base + to, me_head),
            device_id_type=MESH,
        )

    def give_back(g):
        wait_bytes(total_ref.at[g, pl.ds(0, across - 1)], total_sem.at[1, g])
        over_row = decays(row_decay_ref, g)
        carried = jnp.zeros((piece, HD), F32)
        for x in range(across):
            carried = jnp.where(x < me_x, over_row * carried + total_ref[g, x], carried)
        decay = decays(block_decay_ref, g)
        for r in range(ROW):
            back_ref[g, pl.ds(r * piece, piece), :] = carried.astype(BF16)
            carried = decay * carried + rows_ref[g, pl.ds(r * piece, piece), :].astype(F32)

        @pl.loop(1, ROW)
        def _(d):
            back_copy(g, row_peer(d)).start()

        incoming_ref[g, at_piece(me_row), :] = back_ref[g, at_piece(me_row), :]

    def intra(h):
        rows = lax.broadcasted_iota(jnp.int32, (length, length), 0)
        offset = rows - lax.broadcasted_iota(jnp.int32, (length, length), 1)
        decay = jnp.exp(-rate_row(h, length) * jnp.maximum(offset, 0).astype(F32))
        scores = lax.dot_general(
            q_ref[:, head_cols(h)],
            k_ref[:, head_cols(h)],
            (((1,), (1,)), ((), ())),
            preferred_element_type=F32,
        )
        weights = jnp.where(offset >= 0, scores * decay, 0.0).astype(BF16)
        intra_ref[:, head_cols(h)] = jnp.dot(
            weights, v_ref[:, head_cols(h)], preferred_element_type=F32
        )

    def make_pick():
        expert = lax.broadcasted_iota(jnp.int32, (EXPERTS, length), 0)
        named = (routing_ref[0:1, :] == expert) | (routing_ref[1:2, :] == expert)
        named = jnp.where(named, 1.0, 0.0)
        earlier = lax.broadcasted_iota(jnp.int32, (length, length), 0)
        earlier = earlier < lax.broadcasted_iota(jnp.int32, (length, length), 1)
        before = jnp.dot(
            named.astype(BF16), jnp.where(earlier, 1.0, 0.0).astype(BF16), preferred_element_type=F32
        )
        slot = jnp.where(named > 0.5, before, -1.0)
        seat = lax.broadcasted_iota(jnp.int32, (EXPERTS, CAP, length), 1).astype(F32)
        chosen = jnp.where(slot[:, None, :] == seat, 1.0, 0.0)
        pick_ref[...] = chosen.reshape(EXPERTS * CAP, length).astype(BF16)

    def out_copy(g, d):
        return pltpu.make_async_remote_copy(
            src_ref=picked_ref.at[g, d - 1],
            dst_ref=out_ref.at[:, pl.ds(pl.multiple_of(me_head * features + g * width, width), width)],
            send_sem=out_sem.at[0, g],
            recv_sem=out_sem.at[1, g],
            device_id=(seq, head_peer(d)),
            device_id_type=MESH,
        )

    def finish(g):
        wait_bytes(incoming_ref.at[g, others], back_sem.at[1, g])
        parts = []
        for at in range(per_group):
            h = g * per_group + at
            decay_in = jnp.exp(-rate_row(h, HD) * (place + 1.0))
            inter = jnp.dot(
                q_ref[:, head_cols(h)],
                incoming_ref[g, pl.ds(at * HD, HD), :],
                preferred_element_type=F32,
            )
            attended = inter * decay_in + intra_ref[:, head_cols(h)]
            mean = jnp.sum(attended * attended, axis=-1, keepdims=True) * (1.0 / HD)
            normed = attended * lax.rsqrt(mean + 1e-05) * gain_ref[h : h + 1, :]
            parts.append(normed.astype(BF16))
        normed = jnp.concatenate(parts, axis=1)

        def picked(d):
            owner = pl.ds(pl.multiple_of(head_peer(d) * seats, seats), seats)
            return jnp.dot(pick_ref[owner, :], normed, preferred_element_type=F32).astype(BF16)

        for d in range(1, head_count):
            picked_ref[g, d - 1] = picked(d)
            out_copy(g, d).start()
        out_ref[:, pl.ds(pl.multiple_of(me_head * features + g * width, width), width)] = picked(0)

    for g in range(GROUPS):
        for copy in loads[g]:
            copy.wait()
        for at in range(per_group):
            state(g * per_group + at)
        if g == 0:
            pl.semaphore_wait(barrier, ROW - 1 + across - 1 + head_count - 1)
        send_row(g)
    make_pick()
    q_load.wait()

    def intra_group(g):
        for at in range(per_group):
            intra(g * per_group + at)

    intra_group(0)
    sum_row(0)
    intra_group(1)
    give_back(0)
    sum_row(1)
    intra_group(2)
    give_back(1)
    sum_row(2)
    intra_group(3)
    finish(0)
    give_back(2)
    sum_row(3)
    finish(1)
    give_back(3)
    finish(2)
    finish(3)

    for g in range(GROUPS):
        wait_bytes(state_ref.at[g, others], row_sem.at[0, g])
        wait_bytes(total_ref.at[g, pl.ds(0, across - 1)], total_sem.at[0, g])
        wait_bytes(back_ref.at[g, others], back_sem.at[0, g])
        wait_bytes(picked_ref.at[g], out_sem.at[0, g])
        wait_bytes(picked_ref.at[g], out_sem.at[1, g])


def on_device(query, key_rows, value_rows, head_norm_gain, decay_level, routing):
    length, features = query.shape
    heads = decay_level.shape[0]
    seq_count = lax.axis_size("seq")
    head_count = lax.axis_size("head")
    across = seq_count // ROW
    width = features // GROUPS
    piece = width // ROW
    seats = EXPERTS // head_count * CAP
    whole = pl.BlockSpec(memory_space=pltpu.VMEM)
    outside = pl.BlockSpec(memory_space=pltpu.HBM)
    dispatched = pl.pallas_call(
        functools.partial(kernel, (length, heads, seq_count, head_count)),
        out_shape=jax.ShapeDtypeStruct((seats, features * head_count), BF16),
        in_specs=[pl.BlockSpec(memory_space=pltpu.SMEM), whole, whole, outside, outside, outside],
        out_specs=whole,
        scratch_shapes=[
            pltpu.VMEM((length, features), BF16),
            pltpu.VMEM((length, features), BF16),
            pltpu.VMEM((length, features), BF16),
            pltpu.VMEM((GROUPS, width, HD), BF16),
            pltpu.VMEM((GROUPS, width, HD), BF16),
            pltpu.VMEM((GROUPS, across, piece, HD), F32),
            pltpu.VMEM((GROUPS, width, HD), BF16),
            pltpu.VMEM((GROUPS, width, HD), BF16),
            pltpu.VMEM((length, features), F32),
            pltpu.VMEM((EXPERTS * CAP, length), BF16),
            pltpu.VMEM((GROUPS, head_count - 1, seats, width), BF16),
            pltpu.VMEM((heads, 8, HD), F32),
            pltpu.VMEM((heads, 8, HD), F32),
            pltpu.SemaphoreType.DMA((3, GROUPS)),
            pltpu.SemaphoreType.DMA((2, GROUPS)),
            pltpu.SemaphoreType.DMA((2, GROUPS)),
            pltpu.SemaphoreType.DMA((2, GROUPS)),
            pltpu.SemaphoreType.DMA((2, GROUPS)),
        ],
        compiler_params=pltpu.CompilerParams(
            collective_id=0, has_side_effects=True, vmem_limit_bytes=40 << 20
        ),
        name="attend_and_dispatch",
    )(
        decay_level,
        routing.T,
        head_norm_gain.reshape(heads, HD),
        query,
        key_rows,
        value_rows,
    )
    return dispatched.reshape(EXPERTS // head_count, CAP, features * head_count)


def solution(mesh):
    in_specs = (
        P("seq", "head"),
        P("seq", "head"),
        P("seq", "head"),
        P("head"),
        P("head"),
        P("seq", None),
    )
    out_specs = P("head", "seq", None)
    return jax.shard_map(
        on_device, mesh=mesh, in_specs=in_specs, out_specs=out_specs, check_vma=False
    )
```

```python
import functools

import jax
import jax.numpy as jnp
from jax import lax
from jax.experimental import pallas as pl
from jax.experimental.pallas import tpu as pltpu
from jax.sharding import PartitionSpec as P

EXPERTS = 32
CAP = 24
HD = 128
ROW = 16
SIZES = (2, 2, 4, 4, 4)
GROUPS = len(SIZES)
FIRST = tuple(sum(SIZES[:g]) for g in range(GROUPS))
MESH = pl.DeviceIdType.MESH
F32 = jnp.float32
BF16 = jnp.bfloat16


def kernel(
    sizes,
    level_hbm,
    routing_hbm,
    gain_hbm,
    q_hbm,
    k_hbm,
    v_hbm,
    out_ref,
    level_ref,
    routing_ref,
    gain_ref,
    q_ref,
    k_ref,
    v_ref,
    state_ref,
    rows_ref,
    total_ref,
    back_ref,
    incoming_ref,
    intra_ref,
    normed_ref,
    landed_ref,
    pick_ref,
    picked_ref,
    block_decay_ref,
    row_decay_ref,
    small_sem,
    load_sem,
    row_sem,
    total_sem,
    back_sem,
    landed_sem,
    sent_sem,
    out_sem,
):
    length, heads, seq_count, head_count = sizes
    across = seq_count // ROW
    features = heads * HD
    seats = EXPERTS // head_count * CAP

    seq = lax.axis_index("seq")
    me_head = lax.axis_index("head")
    me_row = lax.rem(seq, ROW)
    me_x = lax.div(seq, ROW)
    row_base = me_x * ROW
    up = lax.rem(me_head + 1, head_count)
    down = lax.rem(me_head + head_count - 1, head_count)

    level_load = pltpu.make_async_copy(level_hbm, level_ref, small_sem.at[0])
    level_load.start()
    loads = []
    for g in range(GROUPS):
        cols = pl.ds(FIRST[g] * HD, SIZES[g] * HD)
        pair = [
            pltpu.make_async_copy(k_hbm.at[:, cols], k_ref.at[:, cols], load_sem.at[0, g]),
            pltpu.make_async_copy(v_hbm.at[:, cols], v_ref.at[:, cols], load_sem.at[1, g]),
        ]
        for copy in pair:
            copy.start()
        loads.append(pair)
    routing_load = pltpu.make_async_copy(routing_hbm, routing_ref, small_sem.at[1])
    routing_load.start()
    q_load = pltpu.make_async_copy(q_hbm, q_ref, small_sem.at[2])
    q_load.start()
    gain_load = pltpu.make_async_copy(gain_hbm, gain_ref, small_sem.at[3])
    gain_load.start()

    barrier = pltpu.get_barrier_semaphore()

    def greet(device):
        pl.semaphore_signal(barrier, inc=1, device_id=device, device_id_type=MESH)

    def row_peer(d):
        return lax.rem(me_row + d, ROW)

    def x_peer(d):
        return lax.rem(me_x + d, across)

    @pl.loop(1, ROW)
    def _(d):
        greet((row_base + row_peer(d), me_head))

    for d in range(1, across):
        greet((x_peer(d) * ROW + me_row, me_head))
    greet((seq, up))
    greet((seq, down))

    def rate_row(h, n):
        level = jnp.full((1, n), level_ref[h], jnp.int32)
        return jnp.exp2(level.astype(F32) - 2.0) / (length * seq_count)

    place = lax.broadcasted_iota(jnp.int32, (length, HD), 0).astype(F32)

    def head_cols(h):
        return pl.ds(h * HD, HD)

    def state(h):
        decay_out = jnp.exp(-rate_row(h, HD) * (length - 1.0 - place))
        weighted = (k_ref[:, head_cols(h)].astype(F32) * decay_out).astype(BF16)
        made = lax.dot_general(
            weighted, v_ref[:, head_cols(h)], (((0,), (0,)), ((), ())), preferred_element_type=F32
        )
        state_ref[pl.ds(h * HD, HD), :] = made.astype(BF16)

    def piece_of(g):
        return SIZES[g] * HD // ROW

    def at_piece(g, r):
        rows = piece_of(g)
        return pl.ds(pl.multiple_of(FIRST[g] * HD + r * rows, rows), rows)

    def others(g):
        return pl.ds(FIRST[g] * HD, (ROW - 1) * piece_of(g))

    def wait_bytes(ref, sem):
        pltpu.make_async_copy(ref, ref, sem).wait()

    def row_copy(g, to):
        return pltpu.make_async_remote_copy(
            src_ref=state_ref.at[at_piece(g, to), :],
            dst_ref=rows_ref.at[at_piece(g, me_row), :],
            send_sem=row_sem.at[0, g],
            recv_sem=row_sem.at[1, g],
            device_id=(row_base + to, me_head),
            device_id_type=MESH,
        )

    def send_row(g):
        @pl.loop(1, ROW)
        def _(d):
            row_copy(g, row_peer(d)).start()

        rows_ref[at_piece(g, me_row), :] = state_ref[at_piece(g, me_row), :]

    def decays(ref, g):
        mine = FIRST[g] + lax.div(me_row * piece_of(g), HD)
        return jnp.broadcast_to(ref[mine][0:1], (piece_of(g), HD))

    def at_total(g):
        return pl.ds(FIRST[g] * HD // ROW, piece_of(g))

    def total_copy(g, to):
        return pltpu.make_async_remote_copy(
            src_ref=total_ref.at[me_x, at_total(g)],
            dst_ref=total_ref.at[me_x, at_total(g)],
            send_sem=total_sem.at[0, g],
            recv_sem=total_sem.at[1, g],
            device_id=(to * ROW + me_row, me_head),
            device_id_type=MESH,
        )

    def member(g, r):
        return pl.ds(FIRST[g] * HD + r * piece_of(g), piece_of(g))

    def sum_row(g):
        wait_bytes(rows_ref.at[others(g)], row_sem.at[1, g])
        decay = decays(block_decay_ref, g)
        carried = rows_ref[member(g, 0), :].astype(F32)
        for r in range(1, ROW):
            carried = decay * carried + rows_ref[member(g, r), :].astype(F32)
        total_ref[me_x, at_total(g)] = carried
        for d in range(1, across):
            total_copy(g, x_peer(d)).start()

    def back_copy(g, to):
        return pltpu.make_async_remote_copy(
            src_ref=back_ref.at[at_piece(g, to), :],
            dst_ref=incoming_ref.at[at_piece(g, me_row), :],
            send_sem=back_sem.at[0, g],
            recv_sem=back_sem.at[1, g],
            device_id=(row_base + to, me_head),
            device_id_type=MESH,
        )

    def give_back(g):
        wait_bytes(total_ref.at[pl.ds(0, across - 1), at_total(g)], total_sem.at[1, g])
        over_row = decays(row_decay_ref, g)
        carried = jnp.zeros((piece_of(g), HD), F32)
        for x in range(across):
            carried = jnp.where(x < me_x, over_row * carried + total_ref[x, at_total(g)], carried)
        decay = decays(block_decay_ref, g)
        for r in range(ROW):
            back_ref[member(g, r), :] = carried.astype(BF16)
            carried = decay * carried + rows_ref[member(g, r), :].astype(F32)

        @pl.loop(1, ROW)
        def _(d):
            back_copy(g, row_peer(d)).start()

        incoming_ref[at_piece(g, me_row), :] = back_ref[at_piece(g, me_row), :]

    def intra(h):
        rows = lax.broadcasted_iota(jnp.int32, (length, length), 0)
        offset = rows - lax.broadcasted_iota(jnp.int32, (length, length), 1)
        decay = jnp.exp(-rate_row(h, length) * jnp.maximum(offset, 0).astype(F32))
        scores = lax.dot_general(
            q_ref[:, head_cols(h)],
            k_ref[:, head_cols(h)],
            (((1,), (1,)), ((), ())),
            preferred_element_type=F32,
        )
        weights = jnp.where(offset >= 0, scores * decay, 0.0).astype(BF16)
        intra_ref[:, head_cols(h)] = jnp.dot(
            weights, v_ref[:, head_cols(h)], preferred_element_type=F32
        )

    def make_pick():
        routing_load.wait()
        expert = lax.broadcasted_iota(jnp.int32, (EXPERTS, length), 0)
        named = (routing_ref[0:1, :] == expert) | (routing_ref[1:2, :] == expert)
        named = jnp.where(named, 1.0, 0.0)
        earlier = lax.broadcasted_iota(jnp.int32, (length, length), 0)
        earlier = earlier < lax.broadcasted_iota(jnp.int32, (length, length), 1)
        before = jnp.dot(
            named.astype(BF16), jnp.where(earlier, 1.0, 0.0).astype(BF16), preferred_element_type=F32
        )
        slot = jnp.where(named > 0.5, before, -1.0)
        seat = lax.broadcasted_iota(jnp.int32, (EXPERTS, CAP, length), 1).astype(F32)
        chosen = jnp.where(slot[:, None, :] == seat, 1.0, 0.0)
        pick_ref[...] = chosen.reshape(EXPERTS * CAP, length).astype(BF16)

    def half_cols(g, half):
        return pl.ds((FIRST[g] + half * SIZES[g] // 2) * HD, SIZES[g] // 2 * HD)

    def packed_cols(g):
        return pl.ds(FIRST[g] // 2 * HD, SIZES[g] // 2 * HD)

    def out_cols(g, half, head):
        first = (FIRST[g] + half * SIZES[g] // 2) * HD
        return pl.ds(pl.multiple_of(head * features + first, HD), SIZES[g] // 2 * HD)

    def picked_rows(owner, block):
        rows = pl.ds(pl.multiple_of(owner * seats, seats), seats)
        return jnp.dot(pick_ref[rows, :], block, preferred_element_type=F32).astype(BF16)

    def whole_copy(g, half):
        return pltpu.make_async_remote_copy(
            src_ref=normed_ref.at[:, half_cols(g, half)],
            dst_ref=landed_ref.at[half, :, packed_cols(g)],
            send_sem=sent_sem.at[0],
            recv_sem=landed_sem.at[half, g],
            device_id=(seq, down if half else up),
            device_id_type=MESH,
        )

    def send_picked(g, half, origin, place_at, to):
        pltpu.make_async_remote_copy(
            src_ref=picked_ref.at[place_at, :, packed_cols(g)],
            dst_ref=out_ref.at[:, out_cols(g, half, origin)],
            send_sem=sent_sem.at[1],
            recv_sem=out_sem.at[0],
            device_id=(seq, to),
            device_id_type=MESH,
        ).start()

    def finish(g):
        wait_bytes(incoming_ref.at[others(g)], back_sem.at[1, g])
        for half in range(2):
            for at in range(SIZES[g] // 2):
                h = FIRST[g] + half * SIZES[g] // 2 + at
                decay_in = jnp.exp(-rate_row(h, HD) * (place + 1.0))
                inter = jnp.dot(
                    q_ref[:, head_cols(h)],
                    incoming_ref[pl.ds(h * HD, HD), :],
                    preferred_element_type=F32,
                )
                attended = inter * decay_in + intra_ref[:, head_cols(h)]
                mean = jnp.sum(attended * attended, axis=-1, keepdims=True) * (1.0 / HD)
                normed = attended * lax.rsqrt(mean + 1e-05) * gain_ref[h : h + 1, :]
                normed_ref[:, head_cols(h)] = normed.astype(BF16)
            whole_copy(g, half).start()
        for half, to in ((1, up), (0, down)):
            picked_ref[half, :, packed_cols(g)] = picked_rows(to, normed_ref[:, half_cols(g, half)])
            send_picked(g, half, me_head, half, to)
        for half in range(2):
            out_ref[:, out_cols(g, half, me_head)] = picked_rows(
                me_head, normed_ref[:, half_cols(g, half)]
            )

    def relay(g):
        for half, origin, to in ((0, down, up), (1, up, down)):
            whole_copy(g, half).wait_recv()
            block = landed_ref[half, :, packed_cols(g)]
            picked_ref[2 + half, :, packed_cols(g)] = picked_rows(to, block)
            send_picked(g, half, origin, 2 + half, to)
        for half, origin in ((0, down), (1, up)):
            out_ref[:, out_cols(g, half, origin)] = picked_rows(
                me_head, landed_ref[half, :, packed_cols(g)]
            )

    level_load.wait()
    for g in range(GROUPS):
        for copy in loads[g]:
            copy.wait()
        for at in range(SIZES[g]):
            state(FIRST[g] + at)
        if g == 0:
            pl.semaphore_wait(barrier, ROW - 1 + across - 1 + 2)
        send_row(g)
    for h in range(heads):
        rate = rate_row(h, HD)
        block_decay_ref[h] = jnp.broadcast_to(jnp.exp(-rate * length), (8, HD))
        row_decay_ref[h] = jnp.broadcast_to(jnp.exp(-rate * (length * ROW)), (8, HD))
    make_pick()
    q_load.wait()
    gain_load.wait()

    def intra_group(g):
        for at in range(SIZES[g]):
            intra(FIRST[g] + at)

    sum_row(0)
    intra_group(0)
    sum_row(1)
    intra_group(1)
    intra_group(2)
    give_back(0)
    sum_row(2)
    give_back(1)
    sum_row(3)
    intra_group(3)
    give_back(2)
    finish(0)
    sum_row(4)
    finish(1)
    give_back(3)
    intra_group(4)
    relay(0)
    relay(1)
    finish(2)
    give_back(4)
    finish(3)
    relay(2)
    finish(4)
    relay(3)
    relay(4)

    for g in range(GROUPS):
        wait_bytes(state_ref.at[others(g)], row_sem.at[0, g])
        wait_bytes(total_ref.at[pl.ds(0, across - 1), at_total(g)], total_sem.at[0, g])
        wait_bytes(back_ref.at[others(g)], back_sem.at[0, g])
    wait_bytes(normed_ref, sent_sem.at[0])
    wait_bytes(picked_ref, sent_sem.at[1])
    wait_bytes(out_ref.at[:, pl.ds(0, 2 * features)], out_sem.at[0])


def on_device(query, key_rows, value_rows, head_norm_gain, decay_level, routing):
    length, features = query.shape
    heads = decay_level.shape[0]
    seq_count = lax.axis_size("seq")
    head_count = lax.axis_size("head")
    across = seq_count // ROW
    seats = EXPERTS // head_count * CAP
    outside = pl.BlockSpec(memory_space=pltpu.HBM)
    operands = [
        decay_level,
        routing.T,
        head_norm_gain.reshape(heads, HD),
        query,
        key_rows,
        value_rows,
    ]
    dispatched = pl.pallas_call(
        functools.partial(kernel, (length, heads, seq_count, head_count)),
        out_shape=jax.ShapeDtypeStruct((seats, features * head_count), BF16),
        in_specs=[outside] * len(operands),
        out_specs=pl.BlockSpec(memory_space=pltpu.VMEM),
        scratch_shapes=[
            pltpu.SMEM((heads,), jnp.int32),
            pltpu.VMEM((2, length), jnp.int32),
            pltpu.VMEM((heads, HD), F32),
            pltpu.VMEM((length, features), BF16),
            pltpu.VMEM((length, features), BF16),
            pltpu.VMEM((length, features), BF16),
            pltpu.VMEM((features, HD), BF16),
            pltpu.VMEM((features, HD), BF16),
            pltpu.VMEM((across, features // ROW, HD), F32),
            pltpu.VMEM((features, HD), BF16),
            pltpu.VMEM((features, HD), BF16),
            pltpu.VMEM((length, features), F32),
            pltpu.VMEM((length, features), BF16),
            pltpu.VMEM((2, length, features // 2), BF16),
            pltpu.VMEM((EXPERTS * CAP, length), BF16),
            pltpu.VMEM((4, seats, features // 2), BF16),
            pltpu.VMEM((heads, 8, HD), F32),
            pltpu.VMEM((heads, 8, HD), F32),
            pltpu.SemaphoreType.DMA((4,)),
            pltpu.SemaphoreType.DMA((2, GROUPS)),
            pltpu.SemaphoreType.DMA((2, GROUPS)),
            pltpu.SemaphoreType.DMA((2, GROUPS)),
            pltpu.SemaphoreType.DMA((2, GROUPS)),
            pltpu.SemaphoreType.DMA((2, GROUPS)),
            pltpu.SemaphoreType.DMA((2,)),
            pltpu.SemaphoreType.DMA((1,)),
        ],
        compiler_params=pltpu.CompilerParams(
            collective_id=0, has_side_effects=True, vmem_limit_bytes=40 << 20
        ),
        name="attend_and_dispatch",
    )(*[pltpu.with_memory_space_constraint(x, pltpu.HBM) for x in operands])
    return dispatched.reshape(EXPERTS // head_count, CAP, features * head_count)


def solution(mesh):
    in_specs = (
        P("seq", "head"),
        P("seq", "head"),
        P("seq", "head"),
        P("head"),
        P("head"),
        P("seq", None),
    )
    out_specs = P("head", "seq", None)
    return jax.shard_map(
        on_device, mesh=mesh, in_specs=in_specs, out_specs=out_specs, check_vma=False
    )
```

```python
import functools

import jax
import jax.numpy as jnp
from jax import lax
from jax.experimental import pallas as pl
from jax.experimental.pallas import tpu as pltpu
from jax.sharding import PartitionSpec as P

EXPERTS = 32
CAP = 24
HD = 128
ROW = 16
SIZES = (2, 2, 4, 4, 4)
GROUPS = len(SIZES)
FIRST = tuple(sum(SIZES[:g]) for g in range(GROUPS))
MESH = pl.DeviceIdType.MESH
F32 = jnp.float32
BF16 = jnp.bfloat16


def kernel(
    sizes,
    level_hbm,
    routing_hbm,
    gain_hbm,
    q_hbm,
    k_hbm,
    v_hbm,
    out_ref,
    level_ref,
    routing_ref,
    gain_ref,
    q_ref,
    k_ref,
    v_ref,
    state_ref,
    rows_ref,
    total_ref,
    back_ref,
    incoming_ref,
    intra_ref,
    normed_ref,
    landed_ref,
    pick_ref,
    picked_ref,
    block_decay_ref,
    row_decay_ref,
    small_sem,
    load_sem,
    row_sem,
    total_sem,
    back_sem,
    landed_sem,
    sent_sem,
    out_sem,
):
    length, heads, seq_count, head_count = sizes
    across = seq_count // ROW
    features = heads * HD
    seats = EXPERTS // head_count * CAP

    seq = lax.axis_index("seq")
    me_head = lax.axis_index("head")
    me_row = lax.rem(seq, ROW)
    me_x = lax.div(seq, ROW)
    row_base = me_x * ROW
    up = lax.rem(me_head + 1, head_count)
    down = lax.rem(me_head + head_count - 1, head_count)

    level_load = pltpu.make_async_copy(level_hbm, level_ref, small_sem.at[0])
    level_load.start()
    loads = []
    for g in range(GROUPS):
        cols = pl.ds(FIRST[g] * HD, SIZES[g] * HD)
        pair = [
            pltpu.make_async_copy(k_hbm.at[:, cols], k_ref.at[:, cols], load_sem.at[0, g]),
            pltpu.make_async_copy(v_hbm.at[:, cols], v_ref.at[:, cols], load_sem.at[1, g]),
        ]
        for copy in pair:
            copy.start()
        loads.append(pair)
    routing_load = pltpu.make_async_copy(routing_hbm, routing_ref, small_sem.at[1])
    routing_load.start()
    q_load = pltpu.make_async_copy(q_hbm, q_ref, small_sem.at[2])
    q_load.start()
    gain_load = pltpu.make_async_copy(gain_hbm, gain_ref, small_sem.at[3])
    gain_load.start()

    barrier = pltpu.get_barrier_semaphore()

    def greet(device):
        pl.semaphore_signal(barrier, inc=1, device_id=device, device_id_type=MESH)

    def row_peer(d):
        return lax.rem(me_row + d, ROW)

    def far_first(i):
        return ROW // 2 + lax.div(i + 1, 2) * (1 - 2 * lax.rem(i, 2))

    def x_peer(d):
        return lax.rem(me_x + d, across)

    @pl.loop(1, ROW)
    def _(d):
        greet((row_base + row_peer(d), me_head))

    for d in range(1, across):
        greet((x_peer(d) * ROW + me_row, me_head))
    greet((seq, up))
    greet((seq, down))

    def rate_row(h, n):
        level = jnp.full((1, n), level_ref[h], jnp.int32)
        return jnp.exp2(level.astype(F32) - 2.0) / (length * seq_count)

    place = lax.broadcasted_iota(jnp.int32, (length, HD), 0).astype(F32)

    def head_cols(h):
        return pl.ds(h * HD, HD)

    def state(h):
        decay_out = jnp.exp(-rate_row(h, HD) * (length - 1.0 - place))
        weighted = (k_ref[:, head_cols(h)].astype(F32) * decay_out).astype(BF16)
        made = lax.dot_general(
            weighted, v_ref[:, head_cols(h)], (((0,), (0,)), ((), ())), preferred_element_type=F32
        )
        state_ref[pl.ds(h * HD, HD), :] = made.astype(BF16)

    def piece_of(g):
        return SIZES[g] * HD // ROW

    def at_piece(g, r):
        rows = piece_of(g)
        return pl.ds(pl.multiple_of(FIRST[g] * HD + r * rows, rows), rows)

    def others(g):
        return pl.ds(FIRST[g] * HD, (ROW - 1) * piece_of(g))

    def wait_bytes(ref, sem):
        pltpu.make_async_copy(ref, ref, sem).wait()

    def row_copy(g, to):
        return pltpu.make_async_remote_copy(
            src_ref=state_ref.at[at_piece(g, to), :],
            dst_ref=rows_ref.at[at_piece(g, me_row), :],
            send_sem=row_sem.at[0, g],
            recv_sem=row_sem.at[1, g],
            device_id=(row_base + to, me_head),
            device_id_type=MESH,
        )

    def send_row(g):
        @pl.loop(0, ROW - 1)
        def _(i):
            row_copy(g, row_peer(far_first(i))).start()

        rows_ref[at_piece(g, me_row), :] = state_ref[at_piece(g, me_row), :]

    def decays(ref, g):
        mine = FIRST[g] + lax.div(me_row * piece_of(g), HD)
        return jnp.broadcast_to(ref[mine][0:1], (piece_of(g), HD))

    def at_total(g):
        return pl.ds(FIRST[g] * HD // ROW, piece_of(g))

    def total_copy(g, to):
        return pltpu.make_async_remote_copy(
            src_ref=total_ref.at[me_x, at_total(g)],
            dst_ref=total_ref.at[me_x, at_total(g)],
            send_sem=total_sem.at[0, g],
            recv_sem=total_sem.at[1, g],
            device_id=(to * ROW + me_row, me_head),
            device_id_type=MESH,
        )

    def member(g, r):
        return pl.ds(FIRST[g] * HD + r * piece_of(g), piece_of(g))

    def sum_row(g):
        wait_bytes(rows_ref.at[others(g)], row_sem.at[1, g])
        decay = decays(block_decay_ref, g)
        carried = rows_ref[member(g, 0), :].astype(F32)
        for r in range(1, ROW):
            carried = decay * carried + rows_ref[member(g, r), :].astype(F32)
        total_ref[me_x, at_total(g)] = carried
        for d in range(1, across):
            total_copy(g, x_peer(d)).start()

    def back_copy(g, to):
        return pltpu.make_async_remote_copy(
            src_ref=back_ref.at[at_piece(g, to), :],
            dst_ref=incoming_ref.at[at_piece(g, me_row), :],
            send_sem=back_sem.at[0, g],
            recv_sem=back_sem.at[1, g],
            device_id=(row_base + to, me_head),
            device_id_type=MESH,
        )

    def give_back(g):
        wait_bytes(total_ref.at[pl.ds(0, across - 1), at_total(g)], total_sem.at[1, g])
        over_row = decays(row_decay_ref, g)
        carried = jnp.zeros((piece_of(g), HD), F32)
        for x in range(across):
            carried = jnp.where(x < me_x, over_row * carried + total_ref[x, at_total(g)], carried)
        decay = decays(block_decay_ref, g)
        for r in range(ROW):
            back_ref[member(g, r), :] = carried.astype(BF16)
            carried = decay * carried + rows_ref[member(g, r), :].astype(F32)

        @pl.loop(0, ROW - 1)
        def _(i):
            back_copy(g, row_peer(far_first(i))).start()

        incoming_ref[at_piece(g, me_row), :] = back_ref[at_piece(g, me_row), :]

    def intra(h):
        rows = lax.broadcasted_iota(jnp.int32, (length, length), 0)
        offset = rows - lax.broadcasted_iota(jnp.int32, (length, length), 1)
        decay = jnp.exp(-rate_row(h, length) * jnp.maximum(offset, 0).astype(F32))
        scores = lax.dot_general(
            q_ref[:, head_cols(h)],
            k_ref[:, head_cols(h)],
            (((1,), (1,)), ((), ())),
            preferred_element_type=F32,
        )
        weights = jnp.where(offset >= 0, scores * decay, 0.0).astype(BF16)
        intra_ref[:, head_cols(h)] = jnp.dot(
            weights, v_ref[:, head_cols(h)], preferred_element_type=F32
        )

    def make_pick():
        routing_load.wait()
        expert = lax.broadcasted_iota(jnp.int32, (EXPERTS, length), 0)
        named = (routing_ref[0:1, :] == expert) | (routing_ref[1:2, :] == expert)
        named = jnp.where(named, 1.0, 0.0)
        earlier = lax.broadcasted_iota(jnp.int32, (length, length), 0)
        earlier = earlier < lax.broadcasted_iota(jnp.int32, (length, length), 1)
        before = jnp.dot(
            named.astype(BF16), jnp.where(earlier, 1.0, 0.0).astype(BF16), preferred_element_type=F32
        )
        slot = jnp.where(named > 0.5, before, -1.0)
        seat = lax.broadcasted_iota(jnp.int32, (EXPERTS, CAP, length), 1).astype(F32)
        chosen = jnp.where(slot[:, None, :] == seat, 1.0, 0.0)
        pick_ref[...] = chosen.reshape(EXPERTS * CAP, length).astype(BF16)

    def half_cols(g, half):
        return pl.ds((FIRST[g] + half * SIZES[g] // 2) * HD, SIZES[g] // 2 * HD)

    def packed_cols(g):
        return pl.ds(FIRST[g] // 2 * HD, SIZES[g] // 2 * HD)

    def out_cols(g, half, head):
        first = (FIRST[g] + half * SIZES[g] // 2) * HD
        return pl.ds(pl.multiple_of(head * features + first, HD), SIZES[g] // 2 * HD)

    def picked_rows(owner, block):
        rows = pl.ds(pl.multiple_of(owner * seats, seats), seats)
        return jnp.dot(pick_ref[rows, :], block, preferred_element_type=F32).astype(BF16)

    def whole_copy(g, half):
        return pltpu.make_async_remote_copy(
            src_ref=normed_ref.at[:, half_cols(g, half)],
            dst_ref=landed_ref.at[half, :, packed_cols(g)],
            send_sem=sent_sem.at[0],
            recv_sem=landed_sem.at[half, g],
            device_id=(seq, down if half else up),
            device_id_type=MESH,
        )

    def send_picked(g, half, origin, place_at, to):
        pltpu.make_async_remote_copy(
            src_ref=picked_ref.at[place_at, :, packed_cols(g)],
            dst_ref=out_ref.at[:, out_cols(g, half, origin)],
            send_sem=sent_sem.at[1],
            recv_sem=out_sem.at[0],
            device_id=(seq, to),
            device_id_type=MESH,
        ).start()

    def finish(g):
        wait_bytes(incoming_ref.at[others(g)], back_sem.at[1, g])
        for half in range(2):
            for at in range(SIZES[g] // 2):
                h = FIRST[g] + half * SIZES[g] // 2 + at
                decay_in = jnp.exp(-rate_row(h, HD) * (place + 1.0))
                inter = jnp.dot(
                    q_ref[:, head_cols(h)],
                    incoming_ref[pl.ds(h * HD, HD), :],
                    preferred_element_type=F32,
                )
                attended = inter * decay_in + intra_ref[:, head_cols(h)]
                mean = jnp.sum(attended * attended, axis=-1, keepdims=True) * (1.0 / HD)
                normed = attended * lax.rsqrt(mean + 1e-05) * gain_ref[h : h + 1, :]
                normed_ref[:, head_cols(h)] = normed.astype(BF16)
            whole_copy(g, half).start()
        for half, to in ((1, up), (0, down)):
            picked_ref[half, :, packed_cols(g)] = picked_rows(to, normed_ref[:, half_cols(g, half)])
            send_picked(g, half, me_head, half, to)
        for half in range(2):
            out_ref[:, out_cols(g, half, me_head)] = picked_rows(
                me_head, normed_ref[:, half_cols(g, half)]
            )

    def relay(g):
        for half, origin, to in ((0, down, up), (1, up, down)):
            whole_copy(g, half).wait_recv()
            block = landed_ref[half, :, packed_cols(g)]
            picked_ref[2 + half, :, packed_cols(g)] = picked_rows(to, block)
            send_picked(g, half, origin, 2 + half, to)
        for half, origin in ((0, down), (1, up)):
            out_ref[:, out_cols(g, half, origin)] = picked_rows(
                me_head, landed_ref[half, :, packed_cols(g)]
            )

    def intra_group(g):
        for at in range(SIZES[g]):
            intra(FIRST[g] + at)

    def states(g):
        for copy in loads[g]:
            copy.wait()
        for at in range(SIZES[g]):
            state(FIRST[g] + at)

    level_load.wait()
    states(0)
    pl.semaphore_wait(barrier, ROW - 1 + across - 1 + 2)
    send_row(0)
    states(1)
    send_row(1)
    states(2)
    send_row(2)
    states(3)
    send_row(3)
    for h in range(heads):
        rate = rate_row(h, HD)
        block_decay_ref[h] = jnp.broadcast_to(jnp.exp(-rate * length), (8, HD))
        row_decay_ref[h] = jnp.broadcast_to(jnp.exp(-rate * (length * ROW)), (8, HD))
    make_pick()
    q_load.wait()
    gain_load.wait()
    states(4)
    intra_group(0)
    sum_row(0)
    intra_group(1)
    sum_row(1)
    intra_group(2)
    give_back(0)
    give_back(1)
    send_row(4)
    sum_row(2)
    sum_row(3)
    intra_group(3)
    give_back(2)
    finish(0)
    finish(1)
    give_back(3)
    relay(0)
    relay(1)
    sum_row(4)
    intra_group(4)
    finish(2)
    give_back(4)
    finish(3)
    relay(2)
    finish(4)
    relay(3)
    relay(4)

    for g in range(GROUPS):
        wait_bytes(state_ref.at[others(g)], row_sem.at[0, g])
        wait_bytes(total_ref.at[pl.ds(0, across - 1), at_total(g)], total_sem.at[0, g])
        wait_bytes(back_ref.at[others(g)], back_sem.at[0, g])
    wait_bytes(normed_ref, sent_sem.at[0])
    wait_bytes(picked_ref, sent_sem.at[1])
    wait_bytes(out_ref.at[:, pl.ds(0, 2 * features)], out_sem.at[0])


def on_device(query, key_rows, value_rows, head_norm_gain, decay_level, routing):
    length, features = query.shape
    heads = decay_level.shape[0]
    seq_count = lax.axis_size("seq")
    head_count = lax.axis_size("head")
    across = seq_count // ROW
    seats = EXPERTS // head_count * CAP
    outside = pl.BlockSpec(memory_space=pltpu.HBM)
    operands = [
        decay_level,
        routing.T,
        head_norm_gain.reshape(heads, HD),
        query,
        key_rows,
        value_rows,
    ]
    dispatched = pl.pallas_call(
        functools.partial(kernel, (length, heads, seq_count, head_count)),
        out_shape=jax.ShapeDtypeStruct((seats, features * head_count), BF16),
        in_specs=[outside] * len(operands),
        out_specs=pl.BlockSpec(memory_space=pltpu.VMEM),
        scratch_shapes=[
            pltpu.SMEM((heads,), jnp.int32),
            pltpu.VMEM((2, length), jnp.int32),
            pltpu.VMEM((heads, HD), F32),
            pltpu.VMEM((length, features), BF16),
            pltpu.VMEM((length, features), BF16),
            pltpu.VMEM((length, features), BF16),
            pltpu.VMEM((features, HD), BF16),
            pltpu.VMEM((features, HD), BF16),
            pltpu.VMEM((across, features // ROW, HD), F32),
            pltpu.VMEM((features, HD), BF16),
            pltpu.VMEM((features, HD), BF16),
            pltpu.VMEM((length, features), F32),
            pltpu.VMEM((length, features), BF16),
            pltpu.VMEM((2, length, features // 2), BF16),
            pltpu.VMEM((EXPERTS * CAP, length), BF16),
            pltpu.VMEM((4, seats, features // 2), BF16),
            pltpu.VMEM((heads, 8, HD), F32),
            pltpu.VMEM((heads, 8, HD), F32),
            pltpu.SemaphoreType.DMA((4,)),
            pltpu.SemaphoreType.DMA((2, GROUPS)),
            pltpu.SemaphoreType.DMA((2, GROUPS)),
            pltpu.SemaphoreType.DMA((2, GROUPS)),
            pltpu.SemaphoreType.DMA((2, GROUPS)),
            pltpu.SemaphoreType.DMA((2, GROUPS)),
            pltpu.SemaphoreType.DMA((2,)),
            pltpu.SemaphoreType.DMA((1,)),
        ],
        compiler_params=pltpu.CompilerParams(
            collective_id=0, has_side_effects=True, vmem_limit_bytes=40 << 20
        ),
        name="attend_and_dispatch",
    )(*[pltpu.with_memory_space_constraint(x, pltpu.HBM) for x in operands])
    return dispatched.reshape(EXPERTS // head_count, CAP, features * head_count)


def solution(mesh):
    in_specs = (
        P("seq", "head"),
        P("seq", "head"),
        P("seq", "head"),
        P("head"),
        P("head"),
        P("seq", None),
    )
    out_specs = P("head", "seq", None)
    return jax.shard_map(
        on_device, mesh=mesh, in_specs=in_specs, out_specs=out_specs, check_vma=False
    )
```

```python
import functools

import jax
import jax.numpy as jnp
from jax import lax
from jax.experimental import pallas as pl
from jax.experimental.pallas import tpu as pltpu
from jax.sharding import PartitionSpec as P

EXPERTS = 32
CAP = 24
HD = 128
ROW = 16
SIZES = (2, 2, 4, 4, 4)
GROUPS = len(SIZES)
LENT = 2
FIRST = tuple(sum(SIZES[:g]) for g in range(GROUPS))
MESH = pl.DeviceIdType.MESH
F32 = jnp.float32
BF16 = jnp.bfloat16


def kernel(
    sizes,
    level_hbm,
    routing_hbm,
    gain_hbm,
    q_hbm,
    k_hbm,
    v_hbm,
    out_ref,
    level_ref,
    routing_ref,
    gain_ref,
    q_ref,
    k_ref,
    v_ref,
    state_ref,
    rows_ref,
    total_ref,
    back_ref,
    incoming_ref,
    intra_ref,
    normed_ref,
    landed_ref,
    pick_ref,
    picked_ref,
    lent_ref,
    lent_landed_ref,
    lent_picked_ref,
    lent_rows_ref,
    lent_state_ref,
    lent_gain_ref,
    block_decay_ref,
    row_decay_ref,
    small_sem,
    load_sem,
    row_sem,
    total_sem,
    back_sem,
    landed_sem,
    sent_sem,
    out_sem,
    lent_landed_sem,
    lent_sent_sem,
    lent_rows_sem,
    lent_state_sem,
    lent_gain_sem,
):
    length, heads, seq_count, head_count = sizes
    across = seq_count // ROW
    features = heads * HD
    seats = EXPERTS // head_count * CAP

    seq = lax.axis_index("seq")
    me_head = lax.axis_index("head")
    me_row = lax.rem(seq, ROW)
    me_x = lax.div(seq, ROW)
    row_base = me_x * ROW
    up = lax.rem(me_head + 1, head_count)
    down = lax.rem(me_head + head_count - 1, head_count)
    far = lax.rem(me_head + 2, head_count)
    lent_width = SIZES[LENT] * HD
    lent_half = lent_width // 2

    level_load = pltpu.make_async_copy(level_hbm, level_ref, small_sem.at[0])
    level_load.start()
    loads = []
    for g in range(GROUPS):
        cols = pl.ds(FIRST[g] * HD, SIZES[g] * HD)
        pair = [
            pltpu.make_async_copy(k_hbm.at[:, cols], k_ref.at[:, cols], load_sem.at[0, g]),
            pltpu.make_async_copy(v_hbm.at[:, cols], v_ref.at[:, cols], load_sem.at[1, g]),
        ]
        for copy in pair:
            copy.start()
        loads.append(pair)
    routing_load = pltpu.make_async_copy(routing_hbm, routing_ref, small_sem.at[1])
    routing_load.start()
    q_load = pltpu.make_async_copy(q_hbm, q_ref, small_sem.at[2])
    q_load.start()
    gain_load = pltpu.make_async_copy(gain_hbm, gain_ref, small_sem.at[3])
    gain_load.start()

    barrier = pltpu.get_barrier_semaphore()

    def greet(device):
        pl.semaphore_signal(barrier, inc=1, device_id=device, device_id_type=MESH)

    def row_peer(d):
        return lax.rem(me_row + d, ROW)

    def far_first(i):
        return ROW // 2 + lax.div(i + 1, 2) * (1 - 2 * lax.rem(i, 2))

    def x_peer(d):
        return lax.rem(me_x + d, across)

    @pl.loop(1, ROW)
    def _(d):
        greet((row_base + row_peer(d), me_head))

    for d in range(1, across):
        greet((x_peer(d) * ROW + me_row, me_head))
    greet((seq, up))
    greet((seq, down))
    greet((seq, far))

    def rate_row(h, n):
        level = jnp.full((1, n), level_ref[h], jnp.int32)
        return jnp.exp2(level.astype(F32) - 2.0) / (length * seq_count)

    place = lax.broadcasted_iota(jnp.int32, (length, HD), 0).astype(F32)

    def head_cols(h):
        return pl.ds(h * HD, HD)

    def state(h):
        decay_out = jnp.exp(-rate_row(h, HD) * (length - 1.0 - place))
        weighted = (k_ref[:, head_cols(h)].astype(F32) * decay_out).astype(BF16)
        made = lax.dot_general(
            weighted, v_ref[:, head_cols(h)], (((0,), (0,)), ((), ())), preferred_element_type=F32
        )
        state_ref[pl.ds(h * HD, HD), :] = made.astype(BF16)

    def piece_of(g):
        return SIZES[g] * HD // ROW

    def at_piece(g, r):
        rows = piece_of(g)
        return pl.ds(pl.multiple_of(FIRST[g] * HD + r * rows, rows), rows)

    def others(g):
        return pl.ds(FIRST[g] * HD, (ROW - 1) * piece_of(g))

    def wait_bytes(ref, sem):
        pltpu.make_async_copy(ref, ref, sem).wait()

    def row_copy(g, to):
        return pltpu.make_async_remote_copy(
            src_ref=state_ref.at[at_piece(g, to), :],
            dst_ref=rows_ref.at[at_piece(g, me_row), :],
            send_sem=row_sem.at[0, g],
            recv_sem=row_sem.at[1, g],
            device_id=(row_base + to, me_head),
            device_id_type=MESH,
        )

    def send_row(g):
        @pl.loop(0, ROW - 1)
        def _(i):
            row_copy(g, row_peer(far_first(i))).start()

        rows_ref[at_piece(g, me_row), :] = state_ref[at_piece(g, me_row), :]

    def decays(ref, g):
        mine = FIRST[g] + lax.div(me_row * piece_of(g), HD)
        return jnp.broadcast_to(ref[mine][0:1], (piece_of(g), HD))

    def at_total(g):
        return pl.ds(FIRST[g] * HD // ROW, piece_of(g))

    def total_copy(g, to):
        return pltpu.make_async_remote_copy(
            src_ref=total_ref.at[me_x, at_total(g)],
            dst_ref=total_ref.at[me_x, at_total(g)],
            send_sem=total_sem.at[0, g],
            recv_sem=total_sem.at[1, g],
            device_id=(to * ROW + me_row, me_head),
            device_id_type=MESH,
        )

    def member(g, r):
        return pl.ds(FIRST[g] * HD + r * piece_of(g), piece_of(g))

    def sum_row(g):
        wait_bytes(rows_ref.at[others(g)], row_sem.at[1, g])
        decay = decays(block_decay_ref, g)
        carried = rows_ref[member(g, 0), :].astype(F32)
        for r in range(1, ROW):
            carried = decay * carried + rows_ref[member(g, r), :].astype(F32)
        total_ref[me_x, at_total(g)] = carried
        for d in range(1, across):
            total_copy(g, x_peer(d)).start()

    def back_copy(g, to):
        return pltpu.make_async_remote_copy(
            src_ref=back_ref.at[at_piece(g, to), :],
            dst_ref=incoming_ref.at[at_piece(g, me_row), :],
            send_sem=back_sem.at[0, g],
            recv_sem=back_sem.at[1, g],
            device_id=(row_base + to, me_head),
            device_id_type=MESH,
        )

    def give_back(g):
        wait_bytes(total_ref.at[pl.ds(0, across - 1), at_total(g)], total_sem.at[1, g])
        over_row = decays(row_decay_ref, g)
        carried = jnp.zeros((piece_of(g), HD), F32)
        for x in range(across):
            carried = jnp.where(x < me_x, over_row * carried + total_ref[x, at_total(g)], carried)
        decay = decays(block_decay_ref, g)
        for r in range(ROW):
            back_ref[member(g, r), :] = carried.astype(BF16)
            carried = decay * carried + rows_ref[member(g, r), :].astype(F32)

        @pl.loop(0, ROW - 1)
        def _(i):
            back_copy(g, row_peer(far_first(i))).start()

        incoming_ref[at_piece(g, me_row), :] = back_ref[at_piece(g, me_row), :]

    def intra(h):
        rows = lax.broadcasted_iota(jnp.int32, (length, length), 0)
        offset = rows - lax.broadcasted_iota(jnp.int32, (length, length), 1)
        decay = jnp.exp(-rate_row(h, length) * jnp.maximum(offset, 0).astype(F32))
        scores = lax.dot_general(
            q_ref[:, head_cols(h)],
            k_ref[:, head_cols(h)],
            (((1,), (1,)), ((), ())),
            preferred_element_type=F32,
        )
        weights = jnp.where(offset >= 0, scores * decay, 0.0).astype(BF16)
        intra_ref[:, head_cols(h)] = jnp.dot(
            weights, v_ref[:, head_cols(h)], preferred_element_type=F32
        )

    def make_pick():
        routing_load.wait()
        expert = lax.broadcasted_iota(jnp.int32, (EXPERTS, length), 0)
        named = (routing_ref[0:1, :] == expert) | (routing_ref[1:2, :] == expert)
        named = jnp.where(named, 1.0, 0.0)
        earlier = lax.broadcasted_iota(jnp.int32, (length, length), 0)
        earlier = earlier < lax.broadcasted_iota(jnp.int32, (length, length), 1)
        before = jnp.dot(
            named.astype(BF16), jnp.where(earlier, 1.0, 0.0).astype(BF16), preferred_element_type=F32
        )
        slot = jnp.where(named > 0.5, before, -1.0)
        seat = lax.broadcasted_iota(jnp.int32, (EXPERTS, CAP, length), 1).astype(F32)
        chosen = jnp.where(slot[:, None, :] == seat, 1.0, 0.0)
        pick_ref[...] = chosen.reshape(EXPERTS * CAP, length).astype(BF16)

    def half_cols(g, half):
        return pl.ds((FIRST[g] + half * SIZES[g] // 2) * HD, SIZES[g] // 2 * HD)

    def packed_cols(g):
        return pl.ds(FIRST[g] // 2 * HD, SIZES[g] // 2 * HD)

    def out_cols(g, half, head):
        first = (FIRST[g] + half * SIZES[g] // 2) * HD
        return pl.ds(pl.multiple_of(head * features + first, HD), SIZES[g] // 2 * HD)

    def picked_rows(owner, block):
        rows = pl.ds(pl.multiple_of(owner * seats, seats), seats)
        return jnp.dot(pick_ref[rows, :], block, preferred_element_type=F32).astype(BF16)

    def whole_copy(g, half):
        return pltpu.make_async_remote_copy(
            src_ref=normed_ref.at[:, half_cols(g, half)],
            dst_ref=landed_ref.at[half, :, packed_cols(g)],
            send_sem=sent_sem.at[0],
            recv_sem=landed_sem.at[half, g],
            device_id=(seq, down if half else up),
            device_id_type=MESH,
        )

    def send_picked(g, half, origin, place_at, to):
        pltpu.make_async_remote_copy(
            src_ref=picked_ref.at[place_at, :, packed_cols(g)],
            dst_ref=out_ref.at[:, out_cols(g, half, origin)],
            send_sem=sent_sem.at[1],
            recv_sem=out_sem.at[0],
            device_id=(seq, to),
            device_id_type=MESH,
        ).start()

    def finish(g):
        wait_bytes(incoming_ref.at[others(g)], back_sem.at[1, g])
        if g == LENT:
            for to, way in ((up, 0), (down, 1)):
                state_copy(to, way).start()
        for half in range(2):
            for at in range(SIZES[g] // 2):
                h = FIRST[g] + half * SIZES[g] // 2 + at
                decay_in = jnp.exp(-rate_row(h, HD) * (place + 1.0))
                inter = jnp.dot(
                    q_ref[:, head_cols(h)],
                    incoming_ref[pl.ds(h * HD, HD), :],
                    preferred_element_type=F32,
                )
                attended = inter * decay_in + intra_ref[:, head_cols(h)]
                mean = jnp.sum(attended * attended, axis=-1, keepdims=True) * (1.0 / HD)
                normed = attended * lax.rsqrt(mean + 1e-05) * gain_ref[h : h + 1, :]
                normed_ref[:, head_cols(h)] = normed.astype(BF16)
            if g != LENT:
                whole_copy(g, half).start()
        for half, to in () if g == LENT else ((1, up), (0, down)):
            picked_ref[half, :, packed_cols(g)] = picked_rows(to, normed_ref[:, half_cols(g, half)])
            send_picked(g, half, me_head, half, to)
        for half in range(2):
            out_ref[:, out_cols(g, half, me_head)] = picked_rows(
                me_head, normed_ref[:, half_cols(g, half)]
            )

    def relay(g):
        for half, origin, to in ((0, down, up), (1, up, down)):
            whole_copy(g, half).wait_recv()
            block = landed_ref[half, :, packed_cols(g)]
            picked_ref[2 + half, :, packed_cols(g)] = picked_rows(to, block)
            send_picked(g, half, origin, 2 + half, to)
        for half, origin in ((0, down), (1, up)):
            out_ref[:, out_cols(g, half, origin)] = picked_rows(
                me_head, landed_ref[half, :, packed_cols(g)]
            )

    def lent_cols(half):
        return pl.ds(half * lent_half, lent_half)

    def lent_whole_copy(part, half):
        return pltpu.make_async_remote_copy(
            src_ref=lent_ref.at[part, :, lent_cols(half)],
            dst_ref=lent_landed_ref.at[part, half],
            send_sem=lent_sent_sem.at[0],
            recv_sem=lent_landed_sem.at[part, half],
            device_id=(seq, down if half else up),
            device_id_type=MESH,
        )

    def send_lent(part, half, origin, place_at, to):
        pltpu.make_async_remote_copy(
            src_ref=lent_picked_ref.at[part, place_at],
            dst_ref=lent_rows_ref.at[part, origin, :, lent_cols(half)],
            send_sem=lent_sent_sem.at[1],
            recv_sem=lent_rows_sem.at[0],
            device_id=(seq, to),
            device_id_type=MESH,
        ).start()

    def lend(part):
        for half in range(2):
            for at in range(SIZES[LENT] // 2):
                at = half * SIZES[LENT] // 2 + at
                h = FIRST[LENT] + at
                if part == 0:
                    decay_in = jnp.exp(-rate_row(h, HD) * (place + 1.0))
                    value = q_ref[:, head_cols(h)].astype(F32) * decay_in
                else:
                    value = intra_ref[:, head_cols(h)]
                lent_ref[part, :, head_cols(at)] = value.astype(BF16)
            lent_whole_copy(part, half).start()

    def lend_picked(part):
        for half, to in ((1, up), (0, down)):
            lent_picked_ref[part, half] = picked_rows(to, lent_ref[part, :, lent_cols(half)])
            send_lent(part, half, me_head, half, to)

    def lend_on(part):
        for half, origin, to in ((0, down, up), (1, up, down)):
            lent_whole_copy(part, half).wait_recv()
            block = lent_landed_ref[part, half]
            lent_picked_ref[part, 2 + half] = picked_rows(to, block)
            send_lent(part, half, origin, 2 + half, to)
        for half, origin in ((0, down), (1, up)):
            lent_rows_ref[part, origin, :, lent_cols(half)] = picked_rows(
                me_head, lent_landed_ref[part, half]
            )

    def gain_copy(to):
        return pltpu.make_async_remote_copy(
            src_ref=lent_gain_ref.at[me_head],
            dst_ref=lent_gain_ref.at[me_head],
            send_sem=lent_gain_sem.at[0],
            recv_sem=lent_gain_sem.at[1],
            device_id=(seq, to),
            device_id_type=MESH,
        )

    def lend_gain():
        lent_gain_ref[me_head, pl.ds(0, SIZES[LENT]), :] = gain_ref[pl.ds(FIRST[LENT], SIZES[LENT]), :]
        for to in (up, down, far):
            gain_copy(to).start()

    def state_copy(to, way):
        return pltpu.make_async_remote_copy(
            src_ref=incoming_ref.at[pl.ds(FIRST[LENT] * HD, lent_width)],
            dst_ref=lent_state_ref.at[me_head],
            send_sem=lent_sent_sem.at[2],
            recv_sem=lent_state_sem.at[way],
            device_id=(seq, to),
            device_id_type=MESH,
        )

    def lend_states_on():
        for half, origin, to in ((0, down, up), (1, up, down)):
            state_copy(to, half).wait_recv()
            pltpu.make_async_remote_copy(
                src_ref=lent_state_ref.at[origin, lent_cols(half)],
                dst_ref=lent_state_ref.at[origin, lent_cols(half)],
                send_sem=lent_sent_sem.at[3],
                recv_sem=lent_state_sem.at[2],
                device_id=(seq, to),
                device_id_type=MESH,
            ).start()

    def settle(origin):
        for at in range(SIZES[LENT]):
            inter = jnp.dot(
                lent_rows_ref[0, origin, :, head_cols(at)],
                lent_state_ref[origin, head_cols(at), :],
                preferred_element_type=F32,
            )
            attended = inter + lent_rows_ref[1, origin, :, head_cols(at)].astype(F32)
            mean = jnp.sum(attended * attended, axis=-1, keepdims=True) * (1.0 / HD)
            normed = attended * lax.rsqrt(mean + 1e-05) * lent_gain_ref[origin, at : at + 1, :]
            cols = pl.ds(pl.multiple_of(origin * features + (FIRST[LENT] + at) * HD, HD), HD)
            out_ref[:, cols] = normed.astype(BF16)

    def settle_near():
        wait_bytes(lent_picked_ref, lent_rows_sem.at[0])
        wait_bytes(lent_gain_ref.at[pl.ds(0, head_count - 1)], lent_gain_sem.at[1])
        settle(down)
        settle(up)

    def settle_far():
        wait_bytes(lent_state_ref.at[0], lent_state_sem.at[2])
        settle(far)

    def intra_group(g):
        for at in range(SIZES[g]):
            intra(FIRST[g] + at)

    def wait_load(g):
        for copy in loads[g]:
            copy.wait()

    def states(g):
        for at in range(SIZES[g]):
            state(FIRST[g] + at)

    def make_decays():
        for h in range(heads):
            rate = rate_row(h, HD)
            block_decay_ref[h] = jnp.broadcast_to(jnp.exp(-rate * length), (8, HD))
            row_decay_ref[h] = jnp.broadcast_to(jnp.exp(-rate * (length * ROW)), (8, HD))

    level_load.wait()
    wait_load(0)
    states(0)
    pl.semaphore_wait(barrier, ROW - 1 + across - 1 + 3)
    send_row(0)
    q_load.wait()
    lend(0)
    wait_load(1)
    states(1)
    send_row(1)
    make_pick()
    lend_picked(0)
    wait_load(2)
    intra_group(2)
    lend(1)
    lend_picked(1)
    states(2)
    send_row(2)
    wait_load(3)
    states(3)
    send_row(3)
    make_decays()
    gain_load.wait()
    lend_gain()
    sum_row(0)
    wait_load(4)
    states(4)
    intra_group(0)
    sum_row(1)
    intra_group(1)
    lend_on(0)
    give_back(0)
    give_back(1)
    send_row(4)
    sum_row(2)
    sum_row(3)
    intra_group(3)
    lend_on(1)
    give_back(2)
    finish(0)
    finish(1)
    relay(0)
    give_back(3)
    intra_group(4)
    relay(1)
    sum_row(4)
    finish(2)
    finish(3)
    give_back(4)
    lend_states_on()
    relay(3)
    finish(4)
    relay(4)
    settle_near()
    settle_far()

    for g in range(GROUPS):
        wait_bytes(state_ref.at[others(g)], row_sem.at[0, g])
        wait_bytes(total_ref.at[pl.ds(0, across - 1), at_total(g)], total_sem.at[0, g])
        wait_bytes(back_ref.at[others(g)], back_sem.at[0, g])
    sent = features - lent_width
    wait_bytes(normed_ref.at[:, pl.ds(0, sent)], sent_sem.at[0])
    wait_bytes(picked_ref.at[:, :, pl.ds(0, sent // 2)], sent_sem.at[1])
    wait_bytes(lent_ref, lent_sent_sem.at[0])
    wait_bytes(lent_picked_ref, lent_sent_sem.at[1])
    wait_bytes(lent_state_ref.at[pl.ds(0, 2)], lent_sent_sem.at[2])
    wait_bytes(lent_state_ref.at[0], lent_sent_sem.at[3])
    wait_bytes(lent_gain_ref.at[pl.ds(0, head_count - 1)], lent_gain_sem.at[0])
    wait_bytes(out_ref.at[:, pl.ds(0, 2 * sent)], out_sem.at[0])


def on_device(query, key_rows, value_rows, head_norm_gain, decay_level, routing):
    length, features = query.shape
    heads = decay_level.shape[0]
    seq_count = lax.axis_size("seq")
    head_count = lax.axis_size("head")
    across = seq_count // ROW
    seats = EXPERTS // head_count * CAP
    lent_width = SIZES[LENT] * HD
    outside = pl.BlockSpec(memory_space=pltpu.HBM)
    operands = [
        decay_level,
        routing.T,
        head_norm_gain.reshape(heads, HD),
        query,
        key_rows,
        value_rows,
    ]
    dispatched = pl.pallas_call(
        functools.partial(kernel, (length, heads, seq_count, head_count)),
        out_shape=jax.ShapeDtypeStruct((seats, features * head_count), BF16),
        in_specs=[outside] * len(operands),
        out_specs=pl.BlockSpec(memory_space=pltpu.VMEM),
        scratch_shapes=[
            pltpu.SMEM((heads,), jnp.int32),
            pltpu.VMEM((2, length), jnp.int32),
            pltpu.VMEM((heads, HD), F32),
            pltpu.VMEM((length, features), BF16),
            pltpu.VMEM((length, features), BF16),
            pltpu.VMEM((length, features), BF16),
            pltpu.VMEM((features, HD), BF16),
            pltpu.VMEM((features, HD), BF16),
            pltpu.VMEM((across, features // ROW, HD), F32),
            pltpu.VMEM((features, HD), BF16),
            pltpu.VMEM((features, HD), BF16),
            pltpu.VMEM((length, features), F32),
            pltpu.VMEM((length, features), BF16),
            pltpu.VMEM((2, length, features // 2), BF16),
            pltpu.VMEM((EXPERTS * CAP, length), BF16),
            pltpu.VMEM((4, seats, features // 2), BF16),
            pltpu.VMEM((2, length, lent_width), BF16),
            pltpu.VMEM((2, 2, length, lent_width // 2), BF16),
            pltpu.VMEM((2, 4, seats, lent_width // 2), BF16),
            pltpu.VMEM((2, head_count, seats, lent_width), BF16),
            pltpu.VMEM((head_count, lent_width, HD), BF16),
            pltpu.VMEM((head_count, 8, HD), F32),
            pltpu.VMEM((heads, 8, HD), F32),
            pltpu.VMEM((heads, 8, HD), F32),
            pltpu.SemaphoreType.DMA((4,)),
            pltpu.SemaphoreType.DMA((2, GROUPS)),
            pltpu.SemaphoreType.DMA((2, GROUPS)),
            pltpu.SemaphoreType.DMA((2, GROUPS)),
            pltpu.SemaphoreType.DMA((2, GROUPS)),
            pltpu.SemaphoreType.DMA((2, GROUPS)),
            pltpu.SemaphoreType.DMA((2,)),
            pltpu.SemaphoreType.DMA((1,)),
            pltpu.SemaphoreType.DMA((2, 2)),
            pltpu.SemaphoreType.DMA((4,)),
            pltpu.SemaphoreType.DMA((1,)),
            pltpu.SemaphoreType.DMA((3,)),
            pltpu.SemaphoreType.DMA((2,)),
        ],
        compiler_params=pltpu.CompilerParams(
            collective_id=0, has_side_effects=True, vmem_limit_bytes=40 << 20
        ),
        name="attend_and_dispatch",
    )(*[pltpu.with_memory_space_constraint(x, pltpu.HBM) for x in operands])
    return dispatched.reshape(EXPERTS // head_count, CAP, features * head_count)


def solution(mesh):
    in_specs = (
        P("seq", "head"),
        P("seq", "head"),
        P("seq", "head"),
        P("head"),
        P("head"),
        P("seq", None),
    )
    out_specs = P("head", "seq", None)
    return jax.shard_map(
        on_device, mesh=mesh, in_specs=in_specs, out_specs=out_specs, check_vma=False
    )
```

```python
import functools

import jax
import jax.numpy as jnp
from jax import lax
from jax.experimental import pallas as pl
from jax.experimental.pallas import tpu as pltpu
from jax.sharding import PartitionSpec as P

EXPERTS = 32
CAP = 24
HD = 128
ROW = 16
SIZES = (2, 2, 4, 4, 4)
GROUPS = len(SIZES)
LENT = 2
FIRST = tuple(sum(SIZES[:g]) for g in range(GROUPS))
MESH = pl.DeviceIdType.MESH
F32 = jnp.float32
BF16 = jnp.bfloat16


def kernel(
    sizes,
    level_hbm,
    routing_hbm,
    gain_hbm,
    q_hbm,
    k_hbm,
    v_hbm,
    out_ref,
    level_ref,
    routing_ref,
    gain_ref,
    q_ref,
    k_ref,
    v_ref,
    state_ref,
    rows_ref,
    total_ref,
    back_ref,
    incoming_ref,
    intra_ref,
    normed_ref,
    landed_ref,
    pick_ref,
    picked_ref,
    lent_ref,
    lent_landed_ref,
    lent_picked_ref,
    lent_rows_ref,
    lent_state_ref,
    lent_gain_ref,
    block_decay_ref,
    row_decay_ref,
    small_sem,
    load_sem,
    row_sem,
    total_sem,
    back_sem,
    landed_sem,
    sent_sem,
    out_sem,
    lent_landed_sem,
    lent_sent_sem,
    lent_rows_sem,
    lent_state_sem,
    lent_gain_sem,
):
    length, heads, seq_count, head_count = sizes
    across = seq_count // ROW
    features = heads * HD
    seats = EXPERTS // head_count * CAP

    seq = lax.axis_index("seq")
    me_head = lax.axis_index("head")
    me_row = lax.rem(seq, ROW)
    me_x = lax.div(seq, ROW)
    row_base = me_x * ROW
    up = lax.rem(me_head + 1, head_count)
    down = lax.rem(me_head + head_count - 1, head_count)
    far = lax.rem(me_head + 2, head_count)
    lent_width = SIZES[LENT] * HD
    lent_half = lent_width // 2

    level_load = pltpu.make_async_copy(level_hbm, level_ref, small_sem.at[0])
    level_load.start()
    loads = []
    for g in range(GROUPS):
        cols = pl.ds(FIRST[g] * HD, SIZES[g] * HD)
        pairs = ((k_hbm, k_ref), (v_hbm, v_ref), (q_hbm, q_ref))
        loads.append([
            pltpu.make_async_copy(hbm.at[:, cols], ref.at[:, cols], load_sem.at[at, g])
            for at, (hbm, ref) in enumerate(pairs)
        ])
    routing_load = pltpu.make_async_copy(routing_hbm, routing_ref, small_sem.at[1])
    gain_load = pltpu.make_async_copy(gain_hbm, gain_ref, small_sem.at[2])
    for copy in loads[0][:2]:
        copy.start()
    loads[LENT][2].start()
    routing_load.start()
    for g in range(GROUPS):
        for copy in loads[g][2 * (g == 0) : 2 + (g != LENT)]:
            copy.start()
    gain_load.start()

    barrier = pltpu.get_barrier_semaphore()

    def greet(device):
        pl.semaphore_signal(barrier, inc=1, device_id=device, device_id_type=MESH)

    def far_first(i):
        return ROW // 2 + lax.div(i + 1, 2) * (1 - 2 * lax.rem(i, 2))

    def row_peer(d):
        return lax.rem(me_row + d, ROW)

    def x_peer(d):
        return lax.rem(me_x + d, across)

    @pl.loop(0, ROW - 1)
    def _(i):
        greet((row_base + row_peer(far_first(i)), me_head))

    for d in range(1, across):
        greet((x_peer(d) * ROW + me_row, me_head))
    greet((seq, up))
    greet((seq, down))
    greet((seq, far))

    def rate_row(h, n):
        level = jnp.full((1, n), level_ref[h], jnp.int32)
        return jnp.exp2(level.astype(F32) - 2.0) / (length * seq_count)

    place = lax.broadcasted_iota(jnp.int32, (length, HD), 0).astype(F32)

    def head_cols(h):
        return pl.ds(h * HD, HD)

    def state(h):
        decay_out = jnp.exp(-rate_row(h, HD) * (length - 1.0 - place))
        weighted = (k_ref[:, head_cols(h)].astype(F32) * decay_out).astype(BF16)
        made = lax.dot_general(
            weighted, v_ref[:, head_cols(h)], (((0,), (0,)), ((), ())), preferred_element_type=F32
        )
        state_ref[pl.ds(h * HD, HD), :] = made.astype(BF16)

    def piece_of(g):
        return SIZES[g] * HD // ROW

    def at_piece(g, r):
        rows = piece_of(g)
        return pl.ds(pl.multiple_of(FIRST[g] * HD + r * rows, rows), rows)

    def others(g):
        return pl.ds(FIRST[g] * HD, (ROW - 1) * piece_of(g))

    def wait_bytes(ref, sem):
        pltpu.make_async_copy(ref, ref, sem).wait()

    def row_copy(g, to):
        return pltpu.make_async_remote_copy(
            src_ref=state_ref.at[at_piece(g, to), :],
            dst_ref=rows_ref.at[at_piece(g, me_row), :],
            send_sem=row_sem.at[0, g],
            recv_sem=row_sem.at[1, g],
            device_id=(row_base + to, me_head),
            device_id_type=MESH,
        )

    def send_row(g):
        @pl.loop(0, ROW - 1)
        def _(i):
            row_copy(g, row_peer(far_first(i))).start()

        rows_ref[at_piece(g, me_row), :] = state_ref[at_piece(g, me_row), :]

    def decays(ref, g):
        mine = FIRST[g] + lax.div(me_row * piece_of(g), HD)
        return jnp.broadcast_to(ref[mine][0:1], (piece_of(g), HD))

    def at_total(g):
        return pl.ds(FIRST[g] * HD // ROW, piece_of(g))

    def total_copy(g, to):
        return pltpu.make_async_remote_copy(
            src_ref=total_ref.at[me_x, at_total(g)],
            dst_ref=total_ref.at[me_x, at_total(g)],
            send_sem=total_sem.at[0, g],
            recv_sem=total_sem.at[1, g],
            device_id=(to * ROW + me_row, me_head),
            device_id_type=MESH,
        )

    def member(g, r):
        return pl.ds(FIRST[g] * HD + r * piece_of(g), piece_of(g))

    def sum_row(g):
        wait_bytes(rows_ref.at[others(g)], row_sem.at[1, g])
        decay = decays(block_decay_ref, g)
        carried = rows_ref[member(g, 0), :].astype(F32)
        for r in range(1, ROW):
            carried = decay * carried + rows_ref[member(g, r), :].astype(F32)
        total_ref[me_x, at_total(g)] = carried
        for d in (across // 2, *(d for d in range(1, across) if d != across // 2)):
            total_copy(g, x_peer(d)).start()

    def back_copy(g, to):
        return pltpu.make_async_remote_copy(
            src_ref=back_ref.at[at_piece(g, to), :],
            dst_ref=incoming_ref.at[at_piece(g, me_row), :],
            send_sem=back_sem.at[0, g],
            recv_sem=back_sem.at[1, g],
            device_id=(row_base + to, me_head),
            device_id_type=MESH,
        )

    def give_back(g):
        wait_bytes(total_ref.at[pl.ds(0, across - 1), at_total(g)], total_sem.at[1, g])
        over_row = decays(row_decay_ref, g)
        carried = jnp.zeros((piece_of(g), HD), F32)
        for x in range(across):
            carried = jnp.where(x < me_x, over_row * carried + total_ref[x, at_total(g)], carried)
        decay = decays(block_decay_ref, g)
        for r in range(ROW):
            back_ref[member(g, r), :] = carried.astype(BF16)
            carried = decay * carried + rows_ref[member(g, r), :].astype(F32)

        @pl.loop(0, ROW - 1)
        def _(i):
            back_copy(g, row_peer(far_first(i))).start()

        incoming_ref[at_piece(g, me_row), :] = back_ref[at_piece(g, me_row), :]

    def intra(h):
        rows = lax.broadcasted_iota(jnp.int32, (length, length), 0)
        offset = rows - lax.broadcasted_iota(jnp.int32, (length, length), 1)
        decay = jnp.exp(-rate_row(h, length) * jnp.maximum(offset, 0).astype(F32))
        scores = lax.dot_general(
            q_ref[:, head_cols(h)],
            k_ref[:, head_cols(h)],
            (((1,), (1,)), ((), ())),
            preferred_element_type=F32,
        )
        weights = jnp.where(offset >= 0, scores * decay, 0.0).astype(BF16)
        intra_ref[:, head_cols(h)] = jnp.dot(
            weights, v_ref[:, head_cols(h)], preferred_element_type=F32
        )

    def make_pick():
        routing_load.wait()
        expert = lax.broadcasted_iota(jnp.int32, (EXPERTS, length), 0)
        named = (routing_ref[0:1, :] == expert) | (routing_ref[1:2, :] == expert)
        named = jnp.where(named, 1.0, 0.0)
        earlier = lax.broadcasted_iota(jnp.int32, (length, length), 0)
        earlier = earlier < lax.broadcasted_iota(jnp.int32, (length, length), 1)
        before = jnp.dot(
            named.astype(BF16), jnp.where(earlier, 1.0, 0.0).astype(BF16), preferred_element_type=F32
        )
        slot = jnp.where(named > 0.5, before, -1.0)
        seat = lax.broadcasted_iota(jnp.int32, (EXPERTS, CAP, length), 1).astype(F32)
        chosen = jnp.where(slot[:, None, :] == seat, 1.0, 0.0)
        pick_ref[...] = chosen.reshape(EXPERTS * CAP, length).astype(BF16)

    def half_cols(g, half):
        return pl.ds((FIRST[g] + half * SIZES[g] // 2) * HD, SIZES[g] // 2 * HD)

    def packed_cols(g):
        return pl.ds(FIRST[g] // 2 * HD, SIZES[g] // 2 * HD)

    def out_cols(g, half, head):
        first = (FIRST[g] + half * SIZES[g] // 2) * HD
        return pl.ds(pl.multiple_of(head * features + first, HD), SIZES[g] // 2 * HD)

    def picked_rows(owner, block):
        rows = pl.ds(pl.multiple_of(owner * seats, seats), seats)
        return jnp.dot(pick_ref[rows, :], block, preferred_element_type=F32).astype(BF16)

    def whole_copy(g, half):
        return pltpu.make_async_remote_copy(
            src_ref=normed_ref.at[:, half_cols(g, half)],
            dst_ref=landed_ref.at[half, :, packed_cols(g)],
            send_sem=sent_sem.at[0],
            recv_sem=landed_sem.at[half, g],
            device_id=(seq, down if half else up),
            device_id_type=MESH,
        )

    def send_picked(g, half, origin, place_at, to):
        pltpu.make_async_remote_copy(
            src_ref=picked_ref.at[place_at, :, packed_cols(g)],
            dst_ref=out_ref.at[:, out_cols(g, half, origin)],
            send_sem=sent_sem.at[1],
            recv_sem=out_sem.at[0],
            device_id=(seq, to),
            device_id_type=MESH,
        ).start()

    def finish(g):
        wait_bytes(incoming_ref.at[others(g)], back_sem.at[1, g])
        if g == LENT:
            for to, way in ((up, 0), (down, 1)):
                state_copy(to, way).start()
        for half in range(2):
            for at in range(SIZES[g] // 2):
                h = FIRST[g] + half * SIZES[g] // 2 + at
                decay_in = jnp.exp(-rate_row(h, HD) * (place + 1.0))
                inter = jnp.dot(
                    q_ref[:, head_cols(h)],
                    incoming_ref[pl.ds(h * HD, HD), :],
                    preferred_element_type=F32,
                )
                attended = inter * decay_in + intra_ref[:, head_cols(h)]
                mean = jnp.sum(attended * attended, axis=-1, keepdims=True) * (1.0 / HD)
                normed = attended * lax.rsqrt(mean + 1e-05) * gain_ref[h : h + 1, :]
                normed_ref[:, head_cols(h)] = normed.astype(BF16)
            if g != LENT:
                whole_copy(g, half).start()

    def finish_picked(g):
        for half, to in () if g == LENT else ((1, up), (0, down)):
            picked_ref[half, :, packed_cols(g)] = picked_rows(to, normed_ref[:, half_cols(g, half)])
            send_picked(g, half, me_head, half, to)
        for half in range(2):
            out_ref[:, out_cols(g, half, me_head)] = picked_rows(
                me_head, normed_ref[:, half_cols(g, half)]
            )

    def relay(g):
        for half, origin, to in ((0, down, up), (1, up, down)):
            whole_copy(g, half).wait_recv()
            block = landed_ref[half, :, packed_cols(g)]
            picked_ref[2 + half, :, packed_cols(g)] = picked_rows(to, block)
            send_picked(g, half, origin, 2 + half, to)
        for half, origin in ((0, down), (1, up)):
            out_ref[:, out_cols(g, half, origin)] = picked_rows(
                me_head, landed_ref[half, :, packed_cols(g)]
            )

    def lent_cols(half):
        return pl.ds(half * lent_half, lent_half)

    def lent_whole_copy(part, half):
        return pltpu.make_async_remote_copy(
            src_ref=lent_ref.at[part, :, lent_cols(half)],
            dst_ref=lent_landed_ref.at[part, half],
            send_sem=lent_sent_sem.at[0],
            recv_sem=lent_landed_sem.at[part, half],
            device_id=(seq, down if half else up),
            device_id_type=MESH,
        )

    def send_lent(part, half, origin, place_at, to):
        pltpu.make_async_remote_copy(
            src_ref=lent_picked_ref.at[part, place_at],
            dst_ref=lent_rows_ref.at[part, origin, :, lent_cols(half)],
            send_sem=lent_sent_sem.at[1],
            recv_sem=lent_rows_sem.at[0],
            device_id=(seq, to),
            device_id_type=MESH,
        ).start()

    def lend(part):
        for half in range(2):
            for at in range(SIZES[LENT] // 2):
                at = half * SIZES[LENT] // 2 + at
                h = FIRST[LENT] + at
                if part == 0:
                    decay_in = jnp.exp(-rate_row(h, HD) * (place + 1.0))
                    value = q_ref[:, head_cols(h)].astype(F32) * decay_in
                else:
                    value = intra_ref[:, head_cols(h)]
                lent_ref[part, :, head_cols(at)] = value.astype(BF16)

    def lend_whole(part):
        for half in range(2):
            lent_whole_copy(part, half).start()

    def lend_picked(part):
        for half, to in ((1, up), (0, down)):
            lent_picked_ref[part, half] = picked_rows(to, lent_ref[part, :, lent_cols(half)])
            send_lent(part, half, me_head, half, to)

    def lend_on(part):
        for half, origin, to in ((0, down, up), (1, up, down)):
            lent_whole_copy(part, half).wait_recv()
            block = lent_landed_ref[part, half]
            lent_picked_ref[part, 2 + half] = picked_rows(to, block)
            send_lent(part, half, origin, 2 + half, to)
        for half, origin in ((0, down), (1, up)):
            lent_rows_ref[part, origin, :, lent_cols(half)] = picked_rows(
                me_head, lent_landed_ref[part, half]
            )

    def gain_copy(to):
        return pltpu.make_async_remote_copy(
            src_ref=lent_gain_ref.at[me_head],
            dst_ref=lent_gain_ref.at[me_head],
            send_sem=lent_gain_sem.at[0],
            recv_sem=lent_gain_sem.at[1],
            device_id=(seq, to),
            device_id_type=MESH,
        )

    def lend_gain():
        lent_gain_ref[me_head, pl.ds(0, SIZES[LENT]), :] = gain_ref[pl.ds(FIRST[LENT], SIZES[LENT]), :]
        for to in (up, down, far):
            gain_copy(to).start()

    def state_copy(to, way):
        return pltpu.make_async_remote_copy(
            src_ref=incoming_ref.at[pl.ds(FIRST[LENT] * HD, lent_width)],
            dst_ref=lent_state_ref.at[me_head],
            send_sem=lent_sent_sem.at[2],
            recv_sem=lent_state_sem.at[way],
            device_id=(seq, to),
            device_id_type=MESH,
        )

    def lend_states_on():
        for half, origin, to in ((0, down, up), (1, up, down)):
            state_copy(to, half).wait_recv()
            pltpu.make_async_remote_copy(
                src_ref=lent_state_ref.at[origin, lent_cols(half)],
                dst_ref=lent_state_ref.at[origin, lent_cols(half)],
                send_sem=lent_sent_sem.at[3],
                recv_sem=lent_state_sem.at[2],
                device_id=(seq, to),
                device_id_type=MESH,
            ).start()

    def settle(origin):
        for at in range(SIZES[LENT]):
            inter = jnp.dot(
                lent_rows_ref[0, origin, :, head_cols(at)],
                lent_state_ref[origin, head_cols(at), :],
                preferred_element_type=F32,
            )
            attended = inter + lent_rows_ref[1, origin, :, head_cols(at)].astype(F32)
            mean = jnp.sum(attended * attended, axis=-1, keepdims=True) * (1.0 / HD)
            normed = attended * lax.rsqrt(mean + 1e-05) * lent_gain_ref[origin, at : at + 1, :]
            cols = pl.ds(pl.multiple_of(origin * features + (FIRST[LENT] + at) * HD, HD), HD)
            out_ref[:, cols] = normed.astype(BF16)

    def settle_near():
        wait_bytes(lent_picked_ref, lent_rows_sem.at[0])
        wait_bytes(lent_gain_ref.at[pl.ds(0, head_count - 1)], lent_gain_sem.at[1])
        settle(down)
        settle(up)

    def settle_far():
        wait_bytes(lent_state_ref.at[0], lent_state_sem.at[2])
        settle(far)

    def intra_group(g):
        for at in range(SIZES[g]):
            intra(FIRST[g] + at)

    def wait_load(g):
        for copy in loads[g][:2]:
            copy.wait()

    def states(g):
        for at in range(SIZES[g]):
            state(FIRST[g] + at)

    def make_decays():
        for h in range(heads):
            rate = rate_row(h, HD)
            block_decay_ref[h] = jnp.broadcast_to(jnp.exp(-rate * length), (8, HD))
            row_decay_ref[h] = jnp.broadcast_to(jnp.exp(-rate * (length * ROW)), (8, HD))

    level_load.wait()
    wait_load(0)
    states(0)
    loads[2][2].wait()
    lend(0)
    pl.semaphore_wait(barrier, ROW - 1 + across - 1 + 3)
    lend_whole(0)
    send_row(0)
    wait_load(1)
    states(1)
    send_row(1)
    make_pick()
    lend_picked(0)
    wait_load(2)
    intra_group(2)
    lend(1)
    lend_whole(1)
    lend_picked(1)
    states(2)
    send_row(2)
    wait_load(3)
    states(3)
    send_row(3)
    make_decays()
    gain_load.wait()
    lend_gain()
    sum_row(0)
    wait_load(4)
    states(4)
    loads[0][2].wait()
    intra_group(0)
    sum_row(1)
    loads[1][2].wait()
    intra_group(1)
    lend_on(0)
    give_back(0)
    give_back(1)
    send_row(4)
    sum_row(2)
    sum_row(3)
    loads[3][2].wait()
    intra_group(3)
    lend_on(1)
    give_back(2)
    finish(0)
    finish_picked(0)
    finish(1)
    finish_picked(1)
    give_back(3)
    loads[4][2].wait()
    intra_group(4)
    relay(0)
    sum_row(4)
    finish(2)
    finish_picked(2)
    relay(1)
    finish(3)
    finish_picked(3)
    give_back(4)
    lend_states_on()
    relay(3)
    finish(4)
    finish_picked(4)
    settle_near()
    settle_far()
    relay(4)

    for g in range(GROUPS):
        wait_bytes(state_ref.at[others(g)], row_sem.at[0, g])
        wait_bytes(total_ref.at[pl.ds(0, across - 1), at_total(g)], total_sem.at[0, g])
        wait_bytes(back_ref.at[others(g)], back_sem.at[0, g])
    sent = features - lent_width
    wait_bytes(normed_ref.at[:, pl.ds(0, sent)], sent_sem.at[0])
    wait_bytes(picked_ref.at[:, :, pl.ds(0, sent // 2)], sent_sem.at[1])
    wait_bytes(lent_ref, lent_sent_sem.at[0])
    wait_bytes(lent_picked_ref, lent_sent_sem.at[1])
    wait_bytes(lent_state_ref.at[pl.ds(0, 2)], lent_sent_sem.at[2])
    wait_bytes(lent_state_ref.at[0], lent_sent_sem.at[3])
    wait_bytes(lent_gain_ref.at[pl.ds(0, head_count - 1)], lent_gain_sem.at[0])
    wait_bytes(out_ref.at[:, pl.ds(0, 2 * sent)], out_sem.at[0])


def on_device(query, key_rows, value_rows, head_norm_gain, decay_level, routing):
    length, features = query.shape
    heads = decay_level.shape[0]
    seq_count = lax.axis_size("seq")
    head_count = lax.axis_size("head")
    across = seq_count // ROW
    seats = EXPERTS // head_count * CAP
    lent_width = SIZES[LENT] * HD
    outside = pl.BlockSpec(memory_space=pltpu.HBM)
    operands = [
        decay_level,
        routing.T,
        head_norm_gain.reshape(heads, HD),
        query,
        key_rows,
        value_rows,
    ]
    dispatched = pl.pallas_call(
        functools.partial(kernel, (length, heads, seq_count, head_count)),
        out_shape=jax.ShapeDtypeStruct((seats, features * head_count), BF16),
        in_specs=[outside] * len(operands),
        out_specs=pl.BlockSpec(memory_space=pltpu.VMEM),
        scratch_shapes=[
            pltpu.SMEM((heads,), jnp.int32),
            pltpu.VMEM((2, length), jnp.int32),
            pltpu.VMEM((heads, HD), F32),
            pltpu.VMEM((length, features), BF16),
            pltpu.VMEM((length, features), BF16),
            pltpu.VMEM((length, features), BF16),
            pltpu.VMEM((features, HD), BF16),
            pltpu.VMEM((features, HD), BF16),
            pltpu.VMEM((across, features // ROW, HD), F32),
            pltpu.VMEM((features, HD), BF16),
            pltpu.VMEM((features, HD), BF16),
            pltpu.VMEM((length, features), F32),
            pltpu.VMEM((length, features), BF16),
            pltpu.VMEM((2, length, features // 2), BF16),
            pltpu.VMEM((EXPERTS * CAP, length), BF16),
            pltpu.VMEM((4, seats, features // 2), BF16),
            pltpu.VMEM((2, length, lent_width), BF16),
            pltpu.VMEM((2, 2, length, lent_width // 2), BF16),
            pltpu.VMEM((2, 4, seats, lent_width // 2), BF16),
            pltpu.VMEM((2, head_count, seats, lent_width), BF16),
            pltpu.VMEM((head_count, lent_width, HD), BF16),
            pltpu.VMEM((head_count, 8, HD), F32),
            pltpu.VMEM((heads, 8, HD), F32),
            pltpu.VMEM((heads, 8, HD), F32),
            pltpu.SemaphoreType.DMA((3,)),
            pltpu.SemaphoreType.DMA((3, GROUPS)),
            pltpu.SemaphoreType.DMA((2, GROUPS)),
            pltpu.SemaphoreType.DMA((2, GROUPS)),
            pltpu.SemaphoreType.DMA((2, GROUPS)),
            pltpu.SemaphoreType.DMA((2, GROUPS)),
            pltpu.SemaphoreType.DMA((2,)),
            pltpu.SemaphoreType.DMA((1,)),
            pltpu.SemaphoreType.DMA((2, 2)),
            pltpu.SemaphoreType.DMA((4,)),
            pltpu.SemaphoreType.DMA((1,)),
            pltpu.SemaphoreType.DMA((3,)),
            pltpu.SemaphoreType.DMA((2,)),
        ],
        compiler_params=pltpu.CompilerParams(
            collective_id=0, has_side_effects=True, vmem_limit_bytes=40 << 20
        ),
        name="attend_and_dispatch",
    )(*[pltpu.with_memory_space_constraint(x, pltpu.HBM) for x in operands])
    return dispatched.reshape(EXPERTS // head_count, CAP, features * head_count)


def solution(mesh):
    in_specs = (
        P("seq", "head"),
        P("seq", "head"),
        P("seq", "head"),
        P("head"),
        P("head"),
        P("seq", None),
    )
    out_specs = P("head", "seq", None)
    return jax.shard_map(
        on_device, mesh=mesh, in_specs=in_specs, out_specs=out_specs, check_vma=False
    )
```

```python
import functools

import jax
import jax.numpy as jnp
from jax import lax
from jax.experimental import pallas as pl
from jax.experimental.pallas import tpu as pltpu
from jax.sharding import PartitionSpec as P

EXPERTS = 32
CAP = 24
HD = 128
ROW = 16
SIZES = (2, 2, 4, 4, 4)
GROUPS = len(SIZES)
LENT = 2
FIRST = tuple(sum(SIZES[:g]) for g in range(GROUPS))
MESH = pl.DeviceIdType.MESH
F32 = jnp.float32
BF16 = jnp.bfloat16


def kernel(
    sizes,
    level_hbm,
    routing_hbm,
    gain_hbm,
    q_hbm,
    k_hbm,
    v_hbm,
    out_ref,
    level_ref,
    routing_ref,
    gain_ref,
    q_ref,
    k_ref,
    v_ref,
    state_ref,
    rows_ref,
    total_ref,
    back_ref,
    incoming_ref,
    intra_ref,
    normed_ref,
    landed_ref,
    pick_ref,
    picked_ref,
    lent_ref,
    lent_landed_ref,
    lent_picked_ref,
    lent_rows_ref,
    lent_state_ref,
    lent_gain_ref,
    block_decay_ref,
    row_decay_ref,
    small_sem,
    load_sem,
    row_sem,
    total_sem,
    back_sem,
    landed_sem,
    sent_sem,
    out_sem,
    lent_landed_sem,
    lent_sent_sem,
    lent_rows_sem,
    lent_state_sem,
    lent_gain_sem,
):
    length, heads, seq_count, head_count = sizes
    across = seq_count // ROW
    features = heads * HD
    seats = EXPERTS // head_count * CAP

    seq = lax.axis_index("seq")
    me_head = lax.axis_index("head")
    me_row = lax.rem(seq, ROW)
    me_x = lax.div(seq, ROW)
    row_base = me_x * ROW
    up = lax.rem(me_head + 1, head_count)
    down = lax.rem(me_head + head_count - 1, head_count)
    far = lax.rem(me_head + 2, head_count)
    lent_width = SIZES[LENT] * HD
    lent_half = lent_width // 2

    level_load = pltpu.make_async_copy(level_hbm, level_ref, small_sem.at[0])
    level_load.start()
    loads = []
    for g in range(GROUPS):
        cols = pl.ds(FIRST[g] * HD, SIZES[g] * HD)
        pairs = ((k_hbm, k_ref), (v_hbm, v_ref), (q_hbm, q_ref))
        loads.append([
            pltpu.make_async_copy(hbm.at[:, cols], ref.at[:, cols], load_sem.at[at, g])
            for at, (hbm, ref) in enumerate(pairs)
        ])
    routing_load = pltpu.make_async_copy(routing_hbm, routing_ref, small_sem.at[1])
    gain_load = pltpu.make_async_copy(gain_hbm, gain_ref, small_sem.at[2])
    for copy in loads[0][:2]:
        copy.start()
    loads[LENT][2].start()
    routing_load.start()
    for g in range(GROUPS):
        for copy in loads[g][2 * (g == 0) : 2 + (g != LENT)]:
            copy.start()
    gain_load.start()

    barrier = pltpu.get_barrier_semaphore()

    def greet(device):
        pl.semaphore_signal(barrier, inc=1, device_id=device, device_id_type=MESH)

    def far_first(i):
        return ROW // 2 + lax.div(i + 1, 2) * (1 - 2 * lax.rem(i, 2))

    def row_peer(d):
        return lax.rem(me_row + d, ROW)

    def x_peer(d):
        return lax.rem(me_x + d, across)

    @pl.loop(0, ROW - 1)
    def _(i):
        greet((row_base + row_peer(far_first(i)), me_head))

    for d in range(1, across):
        greet((x_peer(d) * ROW + me_row, me_head))
    greet((seq, up))
    greet((seq, down))
    greet((seq, far))

    def rate_row(h, n):
        level = jnp.full((1, n), level_ref[h], jnp.int32)
        return jnp.exp2(level.astype(F32) - 2.0) / (length * seq_count)

    place = lax.broadcasted_iota(jnp.int32, (length, HD), 0).astype(F32)

    def head_cols(h):
        return pl.ds(h * HD, HD)

    def state(h):
        decay_out = jnp.exp(-rate_row(h, HD) * (length - 1.0 - place))
        weighted = (k_ref[:, head_cols(h)].astype(F32) * decay_out).astype(BF16)
        made = lax.dot_general(
            weighted, v_ref[:, head_cols(h)], (((0,), (0,)), ((), ())), preferred_element_type=F32
        )
        state_ref[pl.ds(h * HD, HD), :] = made.astype(BF16)

    def piece_of(g):
        return SIZES[g] * HD // ROW

    def at_piece(g, r):
        rows = piece_of(g)
        return pl.ds(pl.multiple_of(FIRST[g] * HD + r * rows, rows), rows)

    def others(g):
        return pl.ds(FIRST[g] * HD, (ROW - 1) * piece_of(g))

    def wait_bytes(ref, sem):
        pltpu.make_async_copy(ref, ref, sem).wait()

    def row_copy(g, to):
        return pltpu.make_async_remote_copy(
            src_ref=state_ref.at[at_piece(g, to), :],
            dst_ref=rows_ref.at[at_piece(g, me_row), :],
            send_sem=row_sem.at[0, g],
            recv_sem=row_sem.at[1, g],
            device_id=(row_base + to, me_head),
            device_id_type=MESH,
        )

    def send_row(g):
        @pl.loop(0, ROW - 1)
        def _(i):
            row_copy(g, row_peer(far_first(i))).start()

        rows_ref[at_piece(g, me_row), :] = state_ref[at_piece(g, me_row), :]

    def decays(ref, g):
        mine = FIRST[g] + lax.div(me_row * piece_of(g), HD)
        return jnp.broadcast_to(ref[mine][0:1], (piece_of(g), HD))

    def at_total(g):
        return pl.ds(FIRST[g] * HD // ROW, piece_of(g))

    def total_copy(g, to):
        return pltpu.make_async_remote_copy(
            src_ref=total_ref.at[me_x, at_total(g)],
            dst_ref=total_ref.at[me_x, at_total(g)],
            send_sem=total_sem.at[0, g],
            recv_sem=total_sem.at[1, g],
            device_id=(to * ROW + me_row, me_head),
            device_id_type=MESH,
        )

    def member(g, r):
        return pl.ds(FIRST[g] * HD + r * piece_of(g), piece_of(g))

    def sum_row(g):
        wait_bytes(rows_ref.at[others(g)], row_sem.at[1, g])
        decay = decays(block_decay_ref, g)
        carried = rows_ref[member(g, 0), :].astype(F32)
        for r in range(1, ROW):
            carried = decay * carried + rows_ref[member(g, r), :].astype(F32)
        total_ref[me_x, at_total(g)] = carried
        for d in (across // 2, *(d for d in range(1, across) if d != across // 2)):
            total_copy(g, x_peer(d)).start()

    def back_copy(g, to):
        return pltpu.make_async_remote_copy(
            src_ref=back_ref.at[at_piece(g, to), :],
            dst_ref=incoming_ref.at[at_piece(g, me_row), :],
            send_sem=back_sem.at[0, g],
            recv_sem=back_sem.at[1, g],
            device_id=(row_base + to, me_head),
            device_id_type=MESH,
        )

    def give_back(g):
        wait_bytes(total_ref.at[pl.ds(0, across - 1), at_total(g)], total_sem.at[1, g])
        over_row = decays(row_decay_ref, g)
        carried = jnp.zeros((piece_of(g), HD), F32)
        for x in range(across):
            carried = jnp.where(x < me_x, over_row * carried + total_ref[x, at_total(g)], carried)
        decay = decays(block_decay_ref, g)
        for r in range(ROW):
            back_ref[member(g, r), :] = carried.astype(BF16)
            carried = decay * carried + rows_ref[member(g, r), :].astype(F32)

        @pl.loop(0, ROW - 1)
        def _(i):
            back_copy(g, row_peer(far_first(i))).start()

        incoming_ref[at_piece(g, me_row), :] = back_ref[at_piece(g, me_row), :]

    def intra(h):
        rows = lax.broadcasted_iota(jnp.int32, (length, length), 0)
        offset = rows - lax.broadcasted_iota(jnp.int32, (length, length), 1)
        decay = jnp.exp(-rate_row(h, length) * jnp.maximum(offset, 0).astype(F32))
        scores = lax.dot_general(
            q_ref[:, head_cols(h)],
            k_ref[:, head_cols(h)],
            (((1,), (1,)), ((), ())),
            preferred_element_type=F32,
        )
        weights = jnp.where(offset >= 0, scores * decay, 0.0).astype(BF16)
        intra_ref[:, head_cols(h)] = jnp.dot(
            weights, v_ref[:, head_cols(h)], preferred_element_type=F32
        )

    def make_pick():
        routing_load.wait()
        expert = lax.broadcasted_iota(jnp.int32, (EXPERTS, length), 0)
        named = (routing_ref[0:1, :] == expert) | (routing_ref[1:2, :] == expert)
        named = jnp.where(named, 1.0, 0.0)
        earlier = lax.broadcasted_iota(jnp.int32, (length, length), 0)
        earlier = earlier < lax.broadcasted_iota(jnp.int32, (length, length), 1)
        before = jnp.dot(
            named.astype(BF16), jnp.where(earlier, 1.0, 0.0).astype(BF16), preferred_element_type=F32
        )
        slot = jnp.where(named > 0.5, before, -1.0)
        seat = lax.broadcasted_iota(jnp.int32, (EXPERTS, CAP, length), 1).astype(F32)
        chosen = jnp.where(slot[:, None, :] == seat, 1.0, 0.0)
        pick_ref[...] = chosen.reshape(EXPERTS * CAP, length).astype(BF16)

    def half_cols(g, half):
        return pl.ds((FIRST[g] + half * SIZES[g] // 2) * HD, SIZES[g] // 2 * HD)

    def packed_cols(g):
        return pl.ds(FIRST[g] // 2 * HD, SIZES[g] // 2 * HD)

    def out_cols(g, half, head):
        first = (FIRST[g] + half * SIZES[g] // 2) * HD
        return pl.ds(pl.multiple_of(head * features + first, HD), SIZES[g] // 2 * HD)

    def picked_rows(owner, block):
        rows = pl.ds(pl.multiple_of(owner * seats, seats), seats)
        return jnp.dot(pick_ref[rows, :], block, preferred_element_type=F32).astype(BF16)

    def whole_copy(g, half):
        return pltpu.make_async_remote_copy(
            src_ref=normed_ref.at[:, half_cols(g, half)],
            dst_ref=landed_ref.at[half, :, packed_cols(g)],
            send_sem=sent_sem.at[0],
            recv_sem=landed_sem.at[half, g],
            device_id=(seq, down if half else up),
            device_id_type=MESH,
        )

    def send_picked(g, half, origin, place_at, to):
        pltpu.make_async_remote_copy(
            src_ref=picked_ref.at[place_at, :, packed_cols(g)],
            dst_ref=out_ref.at[:, out_cols(g, half, origin)],
            send_sem=sent_sem.at[1],
            recv_sem=out_sem.at[0],
            device_id=(seq, to),
            device_id_type=MESH,
        ).start()

    def finish(g):
        wait_bytes(incoming_ref.at[others(g)], back_sem.at[1, g])
        if g == LENT:
            for to, way in ((up, 0), (down, 1)):
                state_copy(to, way).start()
        for half in range(2):
            for at in range(SIZES[g] // 2):
                h = FIRST[g] + half * SIZES[g] // 2 + at
                decay_in = jnp.exp(-rate_row(h, HD) * (place + 1.0))
                inter = jnp.dot(
                    q_ref[:, head_cols(h)],
                    incoming_ref[pl.ds(h * HD, HD), :],
                    preferred_element_type=F32,
                )
                attended = inter * decay_in + intra_ref[:, head_cols(h)]
                mean = jnp.sum(attended * attended, axis=-1, keepdims=True) * (1.0 / HD)
                normed = attended * lax.rsqrt(mean + 1e-05) * gain_ref[h : h + 1, :]
                normed_ref[:, head_cols(h)] = normed.astype(BF16)
            if g != LENT:
                whole_copy(g, half).start()

    def finish_picked(g):
        for half, to in () if g == LENT else ((1, up), (0, down)):
            picked_ref[half, :, packed_cols(g)] = picked_rows(to, normed_ref[:, half_cols(g, half)])
            send_picked(g, half, me_head, half, to)
        for half in range(2):
            out_ref[:, out_cols(g, half, me_head)] = picked_rows(
                me_head, normed_ref[:, half_cols(g, half)]
            )

    def relay(g):
        for half, origin, to in ((0, down, up), (1, up, down)):
            whole_copy(g, half).wait_recv()
            block = landed_ref[half, :, packed_cols(g)]
            picked_ref[2 + half, :, packed_cols(g)] = picked_rows(to, block)
            send_picked(g, half, origin, 2 + half, to)
        for half, origin in ((0, down), (1, up)):
            out_ref[:, out_cols(g, half, origin)] = picked_rows(
                me_head, landed_ref[half, :, packed_cols(g)]
            )

    def lent_cols(half):
        return pl.ds(half * lent_half, lent_half)

    def lent_whole_copy(part, half):
        return pltpu.make_async_remote_copy(
            src_ref=lent_ref.at[part, :, lent_cols(half)],
            dst_ref=lent_landed_ref.at[part, half],
            send_sem=lent_sent_sem.at[0],
            recv_sem=lent_landed_sem.at[part, half],
            device_id=(seq, down if half else up),
            device_id_type=MESH,
        )

    def send_lent(part, half, origin, place_at, to):
        pltpu.make_async_remote_copy(
            src_ref=lent_picked_ref.at[part, place_at],
            dst_ref=lent_rows_ref.at[part, origin, :, lent_cols(half)],
            send_sem=lent_sent_sem.at[1],
            recv_sem=lent_rows_sem.at[0],
            device_id=(seq, to),
            device_id_type=MESH,
        ).start()

    def lend(part):
        for half in range(2):
            for at in range(SIZES[LENT] // 2):
                at = half * SIZES[LENT] // 2 + at
                h = FIRST[LENT] + at
                if part == 0:
                    decay_in = jnp.exp(-rate_row(h, HD) * (place + 1.0))
                    value = q_ref[:, head_cols(h)].astype(F32) * decay_in
                else:
                    value = intra_ref[:, head_cols(h)]
                lent_ref[part, :, head_cols(at)] = value.astype(BF16)

    def lend_whole(part):
        for half in range(2):
            lent_whole_copy(part, half).start()

    def lend_picked(part):
        for half, to in ((1, up), (0, down)):
            lent_picked_ref[part, half] = picked_rows(to, lent_ref[part, :, lent_cols(half)])
            send_lent(part, half, me_head, half, to)

    def lend_on(part):
        for half, origin, to in ((0, down, up), (1, up, down)):
            lent_whole_copy(part, half).wait_recv()
            block = lent_landed_ref[part, half]
            lent_picked_ref[part, 2 + half] = picked_rows(to, block)
            send_lent(part, half, origin, 2 + half, to)
        for half, origin in ((0, down), (1, up)):
            lent_rows_ref[part, origin, :, lent_cols(half)] = picked_rows(
                me_head, lent_landed_ref[part, half]
            )

    def gain_copy(to):
        return pltpu.make_async_remote_copy(
            src_ref=lent_gain_ref.at[me_head],
            dst_ref=lent_gain_ref.at[me_head],
            send_sem=lent_gain_sem.at[0],
            recv_sem=lent_gain_sem.at[1],
            device_id=(seq, to),
            device_id_type=MESH,
        )

    def lend_gain():
        lent_gain_ref[me_head, pl.ds(0, SIZES[LENT]), :] = gain_ref[pl.ds(FIRST[LENT], SIZES[LENT]), :]
        for to in (up, down, far):
            gain_copy(to).start()

    def state_copy(to, way):
        return pltpu.make_async_remote_copy(
            src_ref=incoming_ref.at[pl.ds(FIRST[LENT] * HD, lent_width)],
            dst_ref=lent_state_ref.at[me_head],
            send_sem=lent_sent_sem.at[2],
            recv_sem=lent_state_sem.at[way],
            device_id=(seq, to),
            device_id_type=MESH,
        )

    def lend_states_on():
        for half, origin, to in ((0, down, up), (1, up, down)):
            state_copy(to, half).wait_recv()
            pltpu.make_async_remote_copy(
                src_ref=lent_state_ref.at[origin, lent_cols(half)],
                dst_ref=lent_state_ref.at[origin, lent_cols(half)],
                send_sem=lent_sent_sem.at[3],
                recv_sem=lent_state_sem.at[2],
                device_id=(seq, to),
                device_id_type=MESH,
            ).start()

    def settle(origin):
        for at in range(SIZES[LENT]):
            inter = jnp.dot(
                lent_rows_ref[0, origin, :, head_cols(at)],
                lent_state_ref[origin, head_cols(at), :],
                preferred_element_type=F32,
            )
            attended = inter + lent_rows_ref[1, origin, :, head_cols(at)].astype(F32)
            mean = jnp.sum(attended * attended, axis=-1, keepdims=True) * (1.0 / HD)
            normed = attended * lax.rsqrt(mean + 1e-05) * lent_gain_ref[origin, at : at + 1, :]
            cols = pl.ds(pl.multiple_of(origin * features + (FIRST[LENT] + at) * HD, HD), HD)
            out_ref[:, cols] = normed.astype(BF16)

    def settle_near():
        wait_bytes(lent_picked_ref, lent_rows_sem.at[0])
        wait_bytes(lent_gain_ref.at[pl.ds(0, head_count - 1)], lent_gain_sem.at[1])
        settle(down)
        settle(up)

    def settle_far():
        wait_bytes(lent_state_ref.at[0], lent_state_sem.at[2])
        settle(far)

    def intra_group(g):
        for at in range(SIZES[g]):
            intra(FIRST[g] + at)

    def wait_load(g):
        for copy in loads[g][:2]:
            copy.wait()

    def states(g):
        for at in range(SIZES[g]):
            state(FIRST[g] + at)

    def make_decays():
        for h in range(heads):
            rate = rate_row(h, HD)
            block_decay_ref[h] = jnp.broadcast_to(jnp.exp(-rate * length), (8, HD))
            row_decay_ref[h] = jnp.broadcast_to(jnp.exp(-rate * (length * ROW)), (8, HD))

    level_load.wait()
    wait_load(0)
    states(0)
    loads[2][2].wait()
    lend(0)
    pl.semaphore_wait(barrier, ROW - 1 + across - 1 + 3)
    lend_whole(0)
    send_row(0)
    wait_load(1)
    states(1)
    send_row(1)
    make_pick()
    lend_picked(0)
    wait_load(2)
    intra_group(2)
    lend(1)
    lend_whole(1)
    lend_picked(1)
    states(2)
    send_row(2)
    wait_load(3)
    states(3)
    send_row(3)
    make_decays()
    gain_load.wait()
    lend_gain()
    sum_row(0)
    wait_load(4)
    states(4)
    loads[0][2].wait()
    intra_group(0)
    sum_row(1)
    loads[1][2].wait()
    intra_group(1)
    lend_on(0)
    give_back(0)
    give_back(1)
    send_row(4)
    sum_row(2)
    sum_row(3)
    loads[3][2].wait()
    intra_group(3)
    lend_on(1)
    give_back(2)
    finish(0)
    finish_picked(0)
    finish(1)
    finish_picked(1)
    give_back(3)
    loads[4][2].wait()
    intra_group(4)
    relay(0)
    sum_row(4)
    finish(2)
    finish_picked(2)
    relay(1)
    finish(3)
    finish_picked(3)
    give_back(4)
    lend_states_on()
    relay(3)
    finish(4)
    finish_picked(4)
    relay(4)
    settle_near()
    settle_far()

    for g in range(GROUPS):
        wait_bytes(state_ref.at[others(g)], row_sem.at[0, g])
        wait_bytes(total_ref.at[pl.ds(0, across - 1), at_total(g)], total_sem.at[0, g])
        wait_bytes(back_ref.at[others(g)], back_sem.at[0, g])
    sent = features - lent_width
    wait_bytes(normed_ref.at[:, pl.ds(0, sent)], sent_sem.at[0])
    wait_bytes(picked_ref.at[:, :, pl.ds(0, sent // 2)], sent_sem.at[1])
    wait_bytes(lent_ref, lent_sent_sem.at[0])
    wait_bytes(lent_picked_ref, lent_sent_sem.at[1])
    wait_bytes(lent_state_ref.at[pl.ds(0, 2)], lent_sent_sem.at[2])
    wait_bytes(lent_state_ref.at[0], lent_sent_sem.at[3])
    wait_bytes(lent_gain_ref.at[pl.ds(0, head_count - 1)], lent_gain_sem.at[0])
    wait_bytes(out_ref.at[:, pl.ds(0, 2 * sent)], out_sem.at[0])


def on_device(query, key_rows, value_rows, head_norm_gain, decay_level, routing):
    length, features = query.shape
    heads = decay_level.shape[0]
    seq_count = lax.axis_size("seq")
    head_count = lax.axis_size("head")
    across = seq_count // ROW
    seats = EXPERTS // head_count * CAP
    lent_width = SIZES[LENT] * HD
    outside = pl.BlockSpec(memory_space=pltpu.HBM)
    operands = [
        decay_level,
        routing.T,
        head_norm_gain.reshape(heads, HD),
        query,
        key_rows,
        value_rows,
    ]
    dispatched = pl.pallas_call(
        functools.partial(kernel, (length, heads, seq_count, head_count)),
        out_shape=jax.ShapeDtypeStruct((seats, features * head_count), BF16),
        in_specs=[outside] * len(operands),
        out_specs=pl.BlockSpec(memory_space=pltpu.VMEM),
        scratch_shapes=[
            pltpu.SMEM((heads,), jnp.int32),
            pltpu.VMEM((2, length), jnp.int32),
            pltpu.VMEM((heads, HD), F32),
            pltpu.VMEM((length, features), BF16),
            pltpu.VMEM((length, features), BF16),
            pltpu.VMEM((length, features), BF16),
            pltpu.VMEM((features, HD), BF16),
            pltpu.VMEM((features, HD), BF16),
            pltpu.VMEM((across, features // ROW, HD), F32),
            pltpu.VMEM((features, HD), BF16),
            pltpu.VMEM((features, HD), BF16),
            pltpu.VMEM((length, features), F32),
            pltpu.VMEM((length, features), BF16),
            pltpu.VMEM((2, length, features // 2), BF16),
            pltpu.VMEM((EXPERTS * CAP, length), BF16),
            pltpu.VMEM((4, seats, features // 2), BF16),
            pltpu.VMEM((2, length, lent_width), BF16),
            pltpu.VMEM((2, 2, length, lent_width // 2), BF16),
            pltpu.VMEM((2, 4, seats, lent_width // 2), BF16),
            pltpu.VMEM((2, head_count, seats, lent_width), BF16),
            pltpu.VMEM((head_count, lent_width, HD), BF16),
            pltpu.VMEM((head_count, 8, HD), F32),
            pltpu.VMEM((heads, 8, HD), F32),
            pltpu.VMEM((heads, 8, HD), F32),
            pltpu.SemaphoreType.DMA((3,)),
            pltpu.SemaphoreType.DMA((3, GROUPS)),
            pltpu.SemaphoreType.DMA((2, GROUPS)),
            pltpu.SemaphoreType.DMA((2, GROUPS)),
            pltpu.SemaphoreType.DMA((2, GROUPS)),
            pltpu.SemaphoreType.DMA((2, GROUPS)),
            pltpu.SemaphoreType.DMA((2,)),
            pltpu.SemaphoreType.DMA((1,)),
            pltpu.SemaphoreType.DMA((2, 2)),
            pltpu.SemaphoreType.DMA((4,)),
            pltpu.SemaphoreType.DMA((1,)),
            pltpu.SemaphoreType.DMA((3,)),
            pltpu.SemaphoreType.DMA((2,)),
        ],
        compiler_params=pltpu.CompilerParams(
            collective_id=0, has_side_effects=True, vmem_limit_bytes=40 << 20
        ),
        name="attend_and_dispatch",
    )(*[pltpu.with_memory_space_constraint(x, pltpu.HBM) for x in operands])
    return dispatched.reshape(EXPERTS // head_count, CAP, features * head_count)


def solution(mesh):
    in_specs = (
        P("seq", "head"),
        P("seq", "head"),
        P("seq", "head"),
        P("head"),
        P("head"),
        P("seq", None),
    )
    out_specs = P("head", "seq", None)
    return jax.shard_map(
        on_device, mesh=mesh, in_specs=in_specs, out_specs=out_specs, check_vma=False
    )
```
